32 devices in a mesh: survey: 2 (over x), sector: 16 (over z, y, core).
Axes of the slice: x: 2, y: 2, z: 4, core: 2. Of those that a mesh axis runs over, the one named last changes fastest.
Arguments:
- raw_pings: bfloat16 [32, 512, 2, 1024], P('survey', 'sector'), parts along dimension 0, may hold values from -6 to 6
- focus_matrix: bfloat16 [2, 2048, 512], replicated, may hold values from -0.25 to 0.25
- start_angle: int32 [32], P('survey'), parts along dimension 0, may hold values from 0 to 2047
- ping_count: int32 [32], P('survey'), parts along dimension 0, may hold values from 256 to 512, as said below
Outputs:
- coherence: float32 [32, 2048, 1024], P(('survey', 'sector')), parts along dimension 0
- interferogram: bfloat16 [32, 2, 2048, 1024], P(('survey', 'sector')), parts along dimension 0
The draws below stay inside these ranges and needn't reach their ends.
There are 2 independent parts, one for each index of `survey`. The reference program is written for one: setup_inputs(seed, part) draws one part's arguments, and reference() takes and returns one part's arrays. A program takes and returns all parts, laid end to end along the dimension named above; an argument that names none is the same for every part. Nothing has to cross between parts.
Inputs may be any that keep to these rules, and one draw needn't show every extreme that they name: `ping_count`: every value lies between 256 and 512, and at least one sector holds all 512 pings.
All inputs are finite; a program needn't handle non-finite values.
Results may differ from the reference program's by a relative error of at most 0.0057.
Values may be sent and summed in bfloat16 or wider, within the bound.
No kernel may reach another device: no remote copies, remote signals or barrier semaphores. Data moves between devices by JAX's collectives and lax.ppermute only.
A program may use at most 192 MiB of HBM per device.

```python
import jax
import jax.numpy as jnp
from jax import lax

PINGS = 512
AZ = 2048
RANGES = 1024
WIN = 9
SECTORS = 16


def draw_ping_count(key, part):
    base = jax.random.fold_in(key, 7)
    first_key, second_key = jax.random.split(base)
    counts = jax.random.randint(first_key, (SECTORS,), PINGS // 2, PINGS + 1).astype(jnp.int32)
    chosen = jax.random.randint(second_key, (), 0, SECTORS)
    return counts.at[chosen].set(PINGS).astype(jnp.int32)


def touch_ends(result, own_key, low, largest):
    place = [jax.random.randint(jax.random.fold_in(own_key, axis), (), 0, length) for axis, length in enumerate(result.shape)]
    longest = result.shape.index(max(result.shape))
    neighbour = place[:longest] + [(place[longest] + 1) % result.shape[longest]] + place[longest + 1:]
    return result.at[tuple(place)].set(low).at[tuple(neighbour)].set(largest)


def levels(own_key, extent, pieces, low, top_value):
    gain = 1.0
    for position, blocks in pieces:
        heights = jax.random.uniform(jax.random.fold_in(jax.random.fold_in(own_key, 6), position), (blocks,), jnp.float32, low / len(pieces), top_value / len(pieces))
        gain = gain * jnp.repeat(jnp.exp(heights), extent[position] // blocks).reshape((-1,) + (1,) * (len(extent) - 1 - position))
    return gain


def bell_draw(stream_key, dims, deviation, reach, shards=(), kind=jnp.bfloat16):
    values = deviation * jax.random.normal(stream_key, dims, jnp.float32)
    if shards:
        values = values * levels(stream_key, dims, shards, -0.22, 0.18)
    return jnp.clip(values, -reach, reach).astype(kind)


def setup_inputs(seed: int = 0, part: int = 0) -> dict:
    keys = jax.random.split(jax.random.key(seed), 5)
    part_keys = jax.random.split(jax.random.fold_in(keys[4], part), 5)
    raw_pings = bell_draw(part_keys[0], (SECTORS, PINGS, 2, RANGES), 1.0, 6.0, ((1, 16),))
    focus_matrix = bell_draw(keys[1], (2, AZ, PINGS), PINGS ** -0.5, 0.25)
    start_angle = touch_ends(jax.random.randint(part_keys[2], (SECTORS,), 0, AZ), jax.random.fold_in(part_keys[2], 1), 0, AZ - 1).astype(jnp.int32)
    ping_count = draw_ping_count(jax.random.fold_in(jax.random.fold_in(keys[4], part), 71), part)
    return {"raw_pings": raw_pings, "focus_matrix": focus_matrix, "start_angle": start_angle, "ping_count": ping_count}


def focus_sector(raw, angle_step, valid_pings, stacked):
    pings_here = raw.shape[0]
    ranges_here = raw.shape[2]
    columns_count = stacked.shape[0] // 2
    ping_mask = (jnp.arange(pings_here, dtype=jnp.int32) < valid_pings).astype(jnp.bfloat16)
    masked = raw * ping_mask[:, None, None]
    product = jnp.dot(stacked, masked.reshape(pings_here, 2 * ranges_here), preferred_element_type=jnp.float32)
    product = product.reshape(2, columns_count, 2, ranges_here)
    real_part = product[0, :, 0] - product[1, :, 1]
    imag_part = product[0, :, 1] + product[1, :, 0]
    columns = jnp.arange(columns_count, dtype=jnp.int32)
    turn_index = angle_step * columns % columns_count
    phase_turn = 2.0 * jnp.pi / columns_count * turn_index.astype(jnp.float32)
    cosine = jnp.cos(phase_turn)[:, None]
    sine_part = jnp.sin(phase_turn)[:, None]
    mean_power = lax.optimization_barrier(jnp.mean(real_part * real_part + imag_part * imag_part, axis=0))
    inverse_rms = lax.rsqrt(mean_power + 1e-06)
    turned_real = (real_part * cosine + imag_part * sine_part) * inverse_rms
    turned_imag = (imag_part * cosine - real_part * sine_part) * inverse_rms
    return jnp.stack([turned_real, turned_imag], axis=1).astype(jnp.bfloat16)

def window_sum(field, axis, span):
    half_span = span // 2
    length_axis = field.shape[axis]
    widths = [(0, 0)] * field.ndim
    widths[axis] = (half_span, half_span)
    padded = jnp.pad(field, widths)
    total = lax.slice_in_dim(padded, 0, length_axis, axis=axis)
    for offset in range(1, span):
        total = total + lax.slice_in_dim(padded, offset, offset + length_axis, axis=axis)
    return total

def compare(own_image, other_image, span):
    f_real = own_image[:, 0].astype(jnp.float32)
    f_imag = own_image[:, 1].astype(jnp.float32)
    g_real = other_image[:, 0].astype(jnp.float32)
    g_imag = other_image[:, 1].astype(jnp.float32)
    fields = jnp.stack([f_real * g_real + f_imag * g_imag, f_imag * g_real - f_real * g_imag, f_real * f_real + f_imag * f_imag, g_real * g_real + g_imag * g_imag], axis=0)
    looked = window_sum(window_sum(fields, 1, span), 2, span)
    magnitude = jnp.sqrt(looked[0] * looked[0] + looked[1] * looked[1])
    energy = jnp.sqrt(looked[2] * looked[3] + 1e-06)
    coherence = magnitude / energy
    interferogram = (looked[0:2] / float(span * span)).astype(jnp.bfloat16)
    return (coherence, interferogram)

def reference(raw_pings, focus_matrix, start_angle, ping_count):
    stacked = focus_matrix.reshape(2 * AZ, PINGS)
    images = lax.map(lambda items: focus_sector(items[0], items[1], items[2], stacked), (raw_pings, start_angle, ping_count))
    following = jnp.roll(images, -1, axis=0)
    coherence, interferogram = lax.map(lambda pair: compare(pair[0], pair[1], WIN), (images, following))
    return (coherence, interferogram)
```

```python
import functools

import jax
import jax.numpy as jnp
from jax import lax
from jax.experimental import pallas as pl
from jax.experimental.pallas import tpu as pltpu
from jax.sharding import PartitionSpec as P

WIN = 9
LANES = 128
CHUNK = 256
VMEM_LIMIT = 62 * 2**20


def shifted(block, axis, distance):
    devices = range(lax.axis_size(axis))
    route = [((i - distance) % len(devices), i) for i in devices]
    return lax.ppermute(block, axis, route)


def load_operand(xr_ref, xi_ref, xa_ref, xb_ref):
    real, imag = xr_ref[...], xi_ref[...]
    xa_ref[:, :CHUNK] = real
    xa_ref[:, CHUNK:] = imag
    xb_ref[:, :CHUNK] = -imag
    xb_ref[:, CHUNK:] = real


def focus_rows(h_ref, xa_ref, xb_ref, start, rows):
    own = jnp.dot(h_ref[0, pl.ds(start, rows), :], xa_ref[...], preferred_element_type=jnp.float32)
    return own + jnp.dot(h_ref[1, pl.ds(start, rows), :], xb_ref[...], preferred_element_type=jnp.float32)


def focus_kernel(h_ref, xr_ref, xi_ref, out_ref, xa_ref, xb_ref, *, rows):
    load_operand(xr_ref, xi_ref, xa_ref, xb_ref)

    @pl.loop(0, h_ref.shape[1] // rows)
    def _(block):
        start = pl.multiple_of(block * rows, rows)
        product = focus_rows(h_ref, xa_ref, xb_ref, start, rows)
        out_ref[0, pl.ds(start, rows), :] = product[:, :CHUNK]
        out_ref[1, pl.ds(start, rows), :] = product[:, CHUNK:]


def focus(h, pings, rows=512):
    _, columns, depth = h.shape
    chunks = pings.shape[1] // 2 // CHUNK
    return pl.pallas_call(
        functools.partial(focus_kernel, rows=rows),
        grid=(chunks,),
        in_specs=[
            pl.BlockSpec(h.shape, lambda j: (0, 0, 0), pipeline_mode=pl.Buffered(1)),
            pl.BlockSpec((depth, CHUNK), lambda j: (0, j)),
            pl.BlockSpec((depth, CHUNK), lambda j: (0, chunks + j)),
        ],
        out_specs=pl.BlockSpec((2, columns, CHUNK), lambda j: (0, 0, j)),
        out_shape=jax.ShapeDtypeStruct((2, columns, chunks * CHUNK), jnp.float32),
        scratch_shapes=[pltpu.VMEM((depth, 2 * CHUNK), jnp.bfloat16)] * 2,
        compiler_params=pltpu.CompilerParams(vmem_limit_bytes=VMEM_LIMIT),
        cost_estimate=pl.CostEstimate(
            flops=16 * columns * depth * chunks * CHUNK // 2, bytes_accessed=24 * 2**20, transcendentals=0
        ),
        name="focus",
    )(h, pings, pings)


def band(shape, offset, half):
    row = lax.broadcasted_iota(jnp.int32, shape, 0)
    column = lax.broadcasted_iota(jnp.int32, shape, 1)
    return jnp.where(jnp.abs(row - offset - column) <= half, 1.0, 0.0).astype(jnp.bfloat16)


def compare_kernel(
    h_ref, xr_ref, xi_ref, f_ref, turn_ref, coherence_ref, interferogram_ref,
    xa_ref, xb_ref, field_ref, looked_ref, azimuth_ref, range_ref, scale_ref, *, chunks, rows, span
):
    step = pl.program_id(0)
    columns = h_ref.shape[1]
    area = float(span * span)
    halo = 16

    @pl.when(step == 0)
    def _():
        azimuth_ref[...] = band(azimuth_ref.shape, 0, span // 2)
        range_ref[...] = band(range_ref.shape, LANES, span // 2)
        edge = jnp.zeros(looked_ref.shape[:2] + (LANES,), jnp.bfloat16)
        looked_ref[:, :, :LANES] = edge
        looked_ref[:, :, (LANES + chunks * CHUNK):] = edge

    @pl.when(step < chunks)
    def _():
        load_operand(xr_ref, xi_ref, xa_ref, xb_ref)

        def block_fields(block, sums):
            start = pl.multiple_of(block * rows, rows)
            product = focus_rows(h_ref, xa_ref, xb_ref, start, rows)
            here = pl.ds(start, rows)
            f_real, f_imag = f_ref[0, here, :], f_ref[1, here, :]
            g_real, g_imag = product[:, :CHUNK], product[:, CHUNK:]
            cosine = jnp.concatenate([turn_ref[0, here, :]] * (CHUNK // LANES), axis=1)
            sine = jnp.concatenate([turn_ref[1, here, :]] * (CHUNK // LANES), axis=1)
            real = f_real * g_real + f_imag * g_imag
            imag = f_imag * g_real - f_real * g_imag
            f_power = f_real * f_real + f_imag * f_imag
            g_power = g_real * g_real + g_imag * g_imag
            field_ref[0, here, :] = (real * cosine + imag * sine).astype(jnp.bfloat16)
            field_ref[1, here, :] = (imag * cosine - real * sine).astype(jnp.bfloat16)
            field_ref[2, here, :] = f_power.astype(jnp.bfloat16)
            field_ref[3, here, :] = g_power.astype(jnp.bfloat16)
            f_sum, g_sum = sums
            return (
                f_sum + jnp.sum(f_power.reshape(rows // 8, 8, CHUNK), axis=0),
                g_sum + jnp.sum(g_power.reshape(rows // 8, 8, CHUNK), axis=0),
            )

        zero = jnp.zeros((8, CHUNK), jnp.float32)
        f_sum, g_sum = lax.fori_loop(0, columns // rows, block_fields, (zero, zero))
        f_scale = lax.rsqrt(jnp.sum(f_sum, axis=0, keepdims=True) / columns + 1e-06)
        g_scale = lax.rsqrt(jnp.sum(g_sum, axis=0, keepdims=True) / columns + 1e-06)
        scale_ref[0:1, :] = f_scale * g_scale / area
        scale_ref[1:2, :] = f_scale * f_scale / area
        scale_ref[2:3, :] = g_scale * g_scale / area
        lanes = pl.ds(pl.multiple_of(LANES + step * CHUNK, LANES), CHUNK)
        size = azimuth_ref.shape[0]
        stride = size - 2 * halo
        weights = azimuth_ref[...]

        def smooth(start, skip):
            for field in range(4):
                total = jnp.dot(weights, field_ref[field, pl.ds(start, size), :], preferred_element_type=jnp.float32)
                scaled = total * scale_ref[max(field - 1, 0):max(field - 1, 0) + 1, :]
                looked_ref[field, pl.ds(start + skip, size - skip), lanes] = scaled.astype(jnp.bfloat16)[skip:]

        smooth(0, 0)

        @pl.loop(1, (columns - size) // stride + 1)
        def _(block):
            smooth(pl.multiple_of(block * stride, halo), halo)

    @pl.when(step > 0)
    def _():
        lanes = pl.ds(pl.multiple_of((step - 1) * CHUNK, LANES), CHUNK + 2 * LANES)

        @pl.loop(0, columns // rows)
        def _(block):
            here = pl.ds(pl.multiple_of(block * rows, rows), rows)
            real, imag, f_power, g_power = (
                jnp.dot(looked_ref[field, here, lanes], range_ref[...], preferred_element_type=jnp.float32)
                for field in range(4)
            )
            interferogram_ref[0, here, :] = real.astype(jnp.bfloat16)
            interferogram_ref[1, here, :] = imag.astype(jnp.bfloat16)
            power = real * real + imag * imag
            energy = f_power * g_power + 1e-06 / (area * area)
            coherence_ref[here, :] = power * lax.rsqrt(jnp.maximum(power * energy, 1e-37))


def compare(h, pings, own, turn, rows=256):
    _, columns, depth = h.shape
    ranges = pings.shape[1] // 2
    chunks = ranges // CHUNK
    last = chunks - 1
    return pl.pallas_call(
        functools.partial(compare_kernel, chunks=chunks, rows=rows, span=WIN),
        grid=(chunks + 1,),
        in_specs=[
            pl.BlockSpec(h.shape, lambda j: (0, 0, 0), pipeline_mode=pl.Buffered(1)),
            pl.BlockSpec((depth, CHUNK), lambda j: (0, jnp.minimum(j, last))),
            pl.BlockSpec((depth, CHUNK), lambda j: (0, chunks + jnp.minimum(j, last))),
            pl.BlockSpec((2, columns, CHUNK), lambda j: (0, 0, jnp.minimum(j, last))),
            pl.BlockSpec(turn.shape, lambda j: (0, 0, 0), pipeline_mode=pl.Buffered(1)),
        ],
        out_specs=[
            pl.BlockSpec((columns, CHUNK), lambda j: (0, jnp.maximum(j - 1, 0))),
            pl.BlockSpec((2, columns, CHUNK), lambda j: (0, 0, jnp.maximum(j - 1, 0))),
        ],
        out_shape=[
            jax.ShapeDtypeStruct((columns, ranges), jnp.float32),
            jax.ShapeDtypeStruct((2, columns, ranges), jnp.bfloat16),
        ],
        scratch_shapes=[
            pltpu.VMEM((depth, 2 * CHUNK), jnp.bfloat16),
            pltpu.VMEM((depth, 2 * CHUNK), jnp.bfloat16),
            pltpu.VMEM((4, columns, CHUNK), jnp.bfloat16),
            pltpu.VMEM((4, columns, ranges + 2 * LANES), jnp.bfloat16),
            pltpu.VMEM((256, 256), jnp.bfloat16),
            pltpu.VMEM((CHUNK + 2 * LANES, CHUNK), jnp.bfloat16),
            pltpu.VMEM((8, CHUNK), jnp.float32),
        ],
        compiler_params=pltpu.CompilerParams(vmem_limit_bytes=VMEM_LIMIT),
        name="compare",
    )(h, pings, pings, own, turn)


def body(raw_pings, focus_matrix, start_angle, ping_count):
    columns = focus_matrix.shape[1]
    sectors = raw_pings.shape[0]
    position = lax.axis_index("sector")
    received = lax.all_to_all(raw_pings, "sector", split_axis=0, concat_axis=1, tiled=True)[0]
    pings = received.shape[0]
    mask = (jnp.arange(pings, dtype=jnp.int32) < ping_count[position]).astype(jnp.bfloat16)
    own_pings = (received * mask[:, None, None]).reshape(pings, -1)
    other_pings = shifted(own_pings, "sector", -1)
    angle = start_angle[position] - start_angle[(position + 1) % sectors]
    index = (angle * jnp.arange(columns, dtype=jnp.int32)) % columns
    phase = 2.0 * jnp.pi / columns * index.astype(jnp.float32)
    turn = jnp.broadcast_to(jnp.stack([jnp.cos(phase), jnp.sin(phase)])[:, :, None], (2, columns, LANES))
    own = focus(focus_matrix, own_pings)
    coherence, interferogram = compare(focus_matrix, other_pings, own, turn)
    return (coherence[None], interferogram[None])


def solution(mesh):
    return jax.shard_map(
        body,
        mesh=mesh,
        in_specs=(P("survey", "sector", None, None), P(), P("survey"), P("survey")),
        out_specs=(P(("survey", "sector"), None, None), P(("survey", "sector"), None, None, None)),
        check_vma=False,
    )
```

```python
import functools

import jax
import jax.numpy as jnp
from jax import lax
from jax.experimental import pallas as pl
from jax.experimental.pallas import tpu as pltpu
from jax.sharding import PartitionSpec as P

WIN = 9
LANES = 128
CHUNK = 256
VMEM_LIMIT = 62 * 2**20


def shifted(block, axis, distance):
    devices = range(lax.axis_size(axis))
    route = [((i - distance) % len(devices), i) for i in devices]
    return lax.ppermute(block, axis, route)


def load_operand(xr_ref, xi_ref, xa_ref, xb_ref):
    real, imag = xr_ref[...], xi_ref[...]
    xa_ref[:, :CHUNK] = real
    xa_ref[:, CHUNK:] = imag
    xb_ref[:, :CHUNK] = -imag
    xb_ref[:, CHUNK:] = real


def focus_rows(h_ref, xa_ref, xb_ref, start, rows):
    own = jnp.dot(h_ref[0, pl.ds(start, rows), :], xa_ref[...], preferred_element_type=jnp.float32)
    return own + jnp.dot(h_ref[1, pl.ds(start, rows), :], xb_ref[...], preferred_element_type=jnp.float32)


def band(shape, offset, half):
    row = lax.broadcasted_iota(jnp.int32, shape, 0)
    column = lax.broadcasted_iota(jnp.int32, shape, 1)
    return jnp.where(jnp.abs(row - offset - column) <= half, 1.0, 0.0).astype(jnp.bfloat16)


def prepare_windows(azimuth_ref, range_ref, looked_ref):
    azimuth_ref[...] = band(azimuth_ref.shape, 0, WIN // 2)
    range_ref[...] = band(range_ref.shape, LANES, WIN // 2)
    edge = jnp.zeros(looked_ref.shape[:2] + (LANES,), jnp.bfloat16)
    looked_ref[:, :, :LANES] = edge
    looked_ref[:, :, (looked_ref.shape[2] - LANES):] = edge


def azimuth_windows(azimuth_ref, field_ref, looked_ref, step, scales):
    halo = 16
    size = azimuth_ref.shape[0]
    stride = size - 2 * halo
    columns = field_ref.shape[0]
    lanes = pl.ds(pl.multiple_of(LANES + step * CHUNK, LANES), CHUNK)

    def smooth(start, skip):
        total = jnp.dot(azimuth_ref[...], field_ref[pl.ds(start, size), :], preferred_element_type=jnp.float32)
        for field, scale in enumerate(scales):
            scaled = total[:, field * CHUNK:(field + 1) * CHUNK] * scale
            looked_ref[field, pl.ds(start + skip, size - skip), lanes] = scaled.astype(jnp.bfloat16)[skip:]

    smooth(0, 0)

    @pl.loop(1, (columns - size) // stride + 1, unroll=True)
    def _(block):
        smooth(pl.multiple_of(block * stride, halo), halo)


def power_sum(power):
    return jnp.sum(power.reshape(power.shape[0] // 8, 8, power.shape[1]), axis=0)


def inverse_rms(sums, columns):
    return lax.rsqrt(jnp.sum(sums, axis=0, keepdims=True) / columns + 1e-06)


def focus_kernel(
    h_ref, xr_ref, xi_ref, out_ref, inverse_ref, power_ref,
    xa_ref, xb_ref, field_ref, looked_ref, azimuth_ref, range_ref, *, chunks, rows
):
    step = pl.program_id(0)
    columns = h_ref.shape[1]

    @pl.when(step == 0)
    def _():
        prepare_windows(azimuth_ref, range_ref, looked_ref)

    @pl.when(step < chunks)
    def _():
        load_operand(xr_ref, xi_ref, xa_ref, xb_ref)

        def block_fields(block, sums):
            start = pl.multiple_of(block * rows, rows)
            here = pl.ds(start, rows)
            product = focus_rows(h_ref, xa_ref, xb_ref, start, rows)
            real, imag = product[:, :CHUNK], product[:, CHUNK:]
            out_ref[0, here, :] = real
            out_ref[1, here, :] = imag
            power = real * real + imag * imag
            field_ref[here, :] = power.astype(jnp.bfloat16)
            return sums + power_sum(power)

        sums = lax.fori_loop(0, columns // rows, block_fields, jnp.zeros((8, CHUNK), jnp.float32))
        inverse = inverse_rms(sums, columns)
        inverse_ref[...] = jnp.broadcast_to(inverse, inverse_ref.shape)
        azimuth_windows(azimuth_ref, field_ref, looked_ref, step, [inverse * inverse / (WIN * WIN)])

    @pl.when(step > 0)
    def _():
        lanes = pl.ds(pl.multiple_of((step - 1) * CHUNK, LANES), CHUNK + 2 * LANES)

        @pl.loop(0, columns // rows)
        def _(block):
            here = pl.ds(pl.multiple_of(block * rows, rows), rows)
            power_ref[here, :] = jnp.dot(
                looked_ref[0, here, lanes], range_ref[...], preferred_element_type=jnp.float32
            )


def focus(h, pings, rows=2048):
    _, columns, depth = h.shape
    ranges = pings.shape[1] // 2
    chunks = ranges // CHUNK
    last = chunks - 1
    return pl.pallas_call(
        functools.partial(focus_kernel, chunks=chunks, rows=rows),
        grid=(chunks + 1,),
        in_specs=[
            pl.BlockSpec(h.shape, lambda j: (0, 0, 0), pipeline_mode=pl.Buffered(1)),
            pl.BlockSpec((depth, CHUNK), lambda j: (0, jnp.minimum(j, last))),
            pl.BlockSpec((depth, CHUNK), lambda j: (0, chunks + jnp.minimum(j, last))),
        ],
        out_specs=[
            pl.BlockSpec((2, columns, CHUNK), lambda j: (0, 0, jnp.minimum(j, last))),
            pl.BlockSpec((8, CHUNK), lambda j: (0, jnp.minimum(j, last))),
            pl.BlockSpec((columns, CHUNK), lambda j: (0, jnp.maximum(j - 1, 0))),
        ],
        out_shape=[
            jax.ShapeDtypeStruct((2, columns, ranges), jnp.float32),
            jax.ShapeDtypeStruct((8, ranges), jnp.float32),
            jax.ShapeDtypeStruct((columns, ranges), jnp.float32),
        ],
        scratch_shapes=[
            pltpu.VMEM((depth, 2 * CHUNK), jnp.bfloat16),
            pltpu.VMEM((depth, 2 * CHUNK), jnp.bfloat16),
            pltpu.VMEM((columns, CHUNK), jnp.bfloat16),
            pltpu.VMEM((1, columns, ranges + 2 * LANES), jnp.bfloat16),
            pltpu.VMEM((256, 256), jnp.bfloat16),
            pltpu.VMEM((CHUNK + 2 * LANES, CHUNK), jnp.bfloat16),
        ],
        compiler_params=pltpu.CompilerParams(vmem_limit_bytes=VMEM_LIMIT),
        cost_estimate=pl.CostEstimate(
            flops=8 * columns * depth * ranges, bytes_accessed=32 * 2**20, transcendentals=0
        ),
        name="focus",
    )(h, pings, pings)


def compare_kernel(
    h_ref, xr_ref, xi_ref, f_ref, inverse_ref, power_ref, coherence_ref, interferogram_ref,
    xa_ref, xb_ref, field_ref, looked_ref, azimuth_ref, range_ref, *, chunks, rows
):
    step = pl.program_id(0)
    columns = h_ref.shape[1]
    area = float(WIN * WIN)

    @pl.when(step == 0)
    def _():
        prepare_windows(azimuth_ref, range_ref, looked_ref)

    @pl.when(step < chunks)
    def _():
        load_operand(xr_ref, xi_ref, xa_ref, xb_ref)

        def block_fields(block, sums):
            start = pl.multiple_of(block * rows, rows)
            product = focus_rows(h_ref, xa_ref, xb_ref, start, rows)
            here = pl.ds(start, rows)
            f_real, f_imag = f_ref[0, here, :], f_ref[1, here, :]
            g_real, g_imag = product[:, :CHUNK], product[:, CHUNK:]
            power = g_real * g_real + g_imag * g_imag
            field_ref[here, :CHUNK] = (f_real * g_real + f_imag * g_imag).astype(jnp.bfloat16)
            field_ref[here, CHUNK:2 * CHUNK] = (f_imag * g_real - f_real * g_imag).astype(jnp.bfloat16)
            field_ref[here, 2 * CHUNK:] = power.astype(jnp.bfloat16)
            return sums + power_sum(power)

        sums = lax.fori_loop(0, columns // rows, block_fields, jnp.zeros((8, CHUNK), jnp.float32))
        f_scale = inverse_ref[:1, :]
        g_scale = inverse_rms(sums, columns)
        cross = f_scale * g_scale / area
        azimuth_windows(azimuth_ref, field_ref, looked_ref, step, [cross, cross, g_scale * g_scale / area])

    @pl.when(step > 0)
    def _():
        lanes = pl.ds(pl.multiple_of((step - 1) * CHUNK, LANES), CHUNK + 2 * LANES)

        @pl.loop(0, columns // rows)
        def _(block):
            here = pl.ds(pl.multiple_of(block * rows, rows), rows)
            real, imag, g_power = (
                jnp.dot(looked_ref[field, here, lanes], range_ref[...], preferred_element_type=jnp.float32)
                for field in range(3)
            )
            interferogram_ref[0, here, :] = real.astype(jnp.bfloat16)
            interferogram_ref[1, here, :] = imag.astype(jnp.bfloat16)
            power = real * real + imag * imag
            energy = power_ref[here, :] * g_power + 1e-06 / (area * area)
            coherence_ref[here, :] = power * lax.rsqrt(jnp.maximum(power * energy, 1e-37))


def compare(h, pings, own, inverse, power, rows=1024):
    _, columns, depth = h.shape
    ranges = pings.shape[1] // 2
    chunks = ranges // CHUNK
    last = chunks - 1
    return pl.pallas_call(
        functools.partial(compare_kernel, chunks=chunks, rows=rows),
        grid=(chunks + 1,),
        in_specs=[
            pl.BlockSpec(h.shape, lambda j: (0, 0, 0), pipeline_mode=pl.Buffered(1)),
            pl.BlockSpec((depth, CHUNK), lambda j: (0, jnp.minimum(j, last))),
            pl.BlockSpec((depth, CHUNK), lambda j: (0, chunks + jnp.minimum(j, last))),
            pl.BlockSpec((2, columns, CHUNK), lambda j: (0, 0, jnp.minimum(j, last))),
            pl.BlockSpec((8, CHUNK), lambda j: (0, jnp.minimum(j, last))),
            pl.BlockSpec((columns, CHUNK), lambda j: (0, jnp.maximum(j - 1, 0))),
        ],
        out_specs=[
            pl.BlockSpec((columns, CHUNK), lambda j: (0, jnp.maximum(j - 1, 0))),
            pl.BlockSpec((2, columns, CHUNK), lambda j: (0, 0, jnp.maximum(j - 1, 0))),
        ],
        out_shape=[
            jax.ShapeDtypeStruct((columns, ranges), jnp.float32),
            jax.ShapeDtypeStruct((2, columns, ranges), jnp.bfloat16),
        ],
        scratch_shapes=[
            pltpu.VMEM((depth, 2 * CHUNK), jnp.bfloat16),
            pltpu.VMEM((depth, 2 * CHUNK), jnp.bfloat16),
            pltpu.VMEM((columns, 3 * CHUNK), jnp.bfloat16),
            pltpu.VMEM((3, columns, ranges + 2 * LANES), jnp.bfloat16),
            pltpu.VMEM((256, 256), jnp.bfloat16),
            pltpu.VMEM((CHUNK + 2 * LANES, CHUNK), jnp.bfloat16),
        ],
        compiler_params=pltpu.CompilerParams(vmem_limit_bytes=VMEM_LIMIT),
        name="compare",
    )(h, pings, pings, own, inverse, power)


def body(raw_pings, focus_matrix, start_angle, ping_count):
    columns = focus_matrix.shape[1]
    sectors = raw_pings.shape[0]
    position = lax.axis_index("sector")
    received = lax.all_to_all(raw_pings, "sector", split_axis=0, concat_axis=1, tiled=True)[0]
    pings = received.shape[0]
    mask = (jnp.arange(pings, dtype=jnp.int32) < ping_count[position]).astype(jnp.bfloat16)
    angle = start_angle[position] - start_angle[(position + 1) % sectors]
    index = (angle * jnp.arange(columns, dtype=jnp.int32)) % columns
    phase = 2.0 * jnp.pi / columns * index.astype(jnp.float32)
    cosine, sine = jnp.cos(phase)[:, None], jnp.sin(phase)[:, None]
    h_real, h_imag = focus_matrix[0].astype(jnp.float32), focus_matrix[1].astype(jnp.float32)
    turned = jnp.stack([h_real * cosine - h_imag * sine, h_real * sine + h_imag * cosine]).astype(jnp.bfloat16)
    received, turned, mask = lax.optimization_barrier((received, turned, mask))
    own_pings = (received * mask[:, None, None]).reshape(pings, -1)
    other_pings = shifted(own_pings, "sector", -1)
    own, inverse, power = focus(focus_matrix, own_pings)
    coherence, interferogram = compare(turned, other_pings, own, inverse, power)
    return (coherence[None], interferogram[None])


def solution(mesh):
    return jax.shard_map(
        body,
        mesh=mesh,
        in_specs=(P("survey", "sector", None, None), P(), P("survey"), P("survey")),
        out_specs=(P(("survey", "sector"), None, None), P(("survey", "sector"), None, None, None)),
        check_vma=False,
    )
```

```python
import functools

import jax
import jax.numpy as jnp
from jax import lax
from jax.experimental import pallas as pl
from jax.experimental.pallas import tpu as pltpu
from jax.sharding import PartitionSpec as P

WIN = 9
LANES = 128
CHUNK = 256
FOCUS_VMEM = 34 * 2**20
COMPARE_VMEM = 48 * 2**20
PART = 512


def shifted(block, axis, distance):
    devices = range(lax.axis_size(axis))
    route = [((i - distance) % len(devices), i) for i in devices]
    return lax.ppermute(block, axis, route)


def load_operand(count_ref, xr_ref, xi_ref, operand_ref):
    depth = xr_ref.shape[0]
    ping = lax.broadcasted_iota(jnp.int32, xr_ref.shape, 0)
    valid = jnp.where(ping < count_ref[0], 1.0, 0.0).astype(jnp.bfloat16)
    real, imag = xr_ref[...] * valid, xi_ref[...] * valid
    operand_ref[:depth, :CHUNK] = real
    operand_ref[:depth, CHUNK:] = imag
    operand_ref[depth:, :CHUNK] = -imag
    operand_ref[depth:, CHUNK:] = real


def band(weights_ref):
    size = weights_ref.shape[1]
    half = WIN // 2
    row = lax.broadcasted_iota(jnp.int32, (size, size), 0)
    column = lax.broadcasted_iota(jnp.int32, (size, size), 1)
    away = jnp.abs(row - column)
    plain = away <= half
    circular = plain | (away >= size - half)
    halves = plain & ((row < LANES) == (column < LANES))
    for index, kept in enumerate((plain, circular, halves)):
        weights_ref[index] = jnp.where(kept, 1.0, 0.0).astype(jnp.bfloat16)


def azimuth_windows(weights_ref, field_ref, looked_ref, tail_ref, step, scales):
    halo = 16
    size = weights_ref.shape[1]
    stride = size - 2 * halo
    columns = field_ref.shape[0]
    blocks = (columns - size) // stride + 1
    base = pl.multiple_of(step * CHUNK, CHUNK)
    for block in range(blocks):
        start = block * stride
        low = halo if block else 0
        high = size if block == blocks - 1 else size - halo
        here = pl.ds(start + low, high - low)
        total = jnp.dot(weights_ref[0], field_ref[pl.ds(start, size), :], preferred_element_type=jnp.float32)
        lane = lax.broadcasted_iota(jnp.int32, (high - low, LANES), 1)
        current = lane < LANES - (WIN - 1) * step
        for field, scale in enumerate(scales):
            scaled = total[low:high, field * CHUNK:(field + 1) * CHUNK] * scale
            last = scaled[:, LANES:]
            before = tail_ref[here, field * LANES:(field + 1) * LANES].astype(jnp.float32)
            looked_ref[field, here, pl.ds(base, LANES)] = scaled[:, :LANES].astype(jnp.bfloat16)
            looked_ref[field, here, pl.ds(base + LANES, LANES)] = jnp.where(current, last, before).astype(jnp.bfloat16)
            tail_ref[here, field * LANES:(field + 1) * LANES] = last.astype(jnp.bfloat16)


def range_windows(weights_ref, looked_ref, tail_ref, here, chunks):
    def product(operand, weights):
        return jnp.dot(operand, weights, preferred_element_type=jnp.float32)

    fields = looked_ref.shape[0]
    following = []
    for field in range(0, fields, 2):
        width = LANES * min(2, fields - field)
        edge = product(tail_ref[here, field * LANES:field * LANES + width], weights_ref[2, :width, :width])
        following += [edge[:, start:start + LANES] for start in range(0, width, LANES)]
    lane = lax.broadcasted_iota(jnp.int32, following[0].shape, 1)
    for chunk in reversed(range(chunks)):
        passes = [
            product(looked_ref[field, here, chunk * CHUNK:(chunk + 1) * CHUNK], weights_ref[1 if chunk else 0])
            for field in range(fields)
        ]
        current = lane < LANES - WIN // 2 - (WIN - 1) * chunk
        after = [jnp.where(current, value[:, LANES:], other) for value, other in zip(passes, following)]
        following = [value[:, LANES:] for value in passes]
        yield 2 * chunk + 1, after
        yield 2 * chunk, [value[:, :LANES] for value in passes]


def power_sum(power):
    return jnp.sum(power.reshape(power.shape[0] // 8, 8, power.shape[1]), axis=0)


def inverse_rms(sums, columns):
    return lax.rsqrt(jnp.sum(sums, axis=0, keepdims=True) / columns + 1e-06)


def focus_kernel(
    count_ref, h_ref, xr_ref, xi_ref, out_ref, inverse_ref, power_ref,
    operand_ref, field_ref, looked_ref, tail_ref, weights_ref, *, chunks, rows
):
    step = pl.program_id(0)
    columns = h_ref.shape[0]

    @pl.when(step == 0)
    def _():
        band(weights_ref)
        tail_ref[...] = jnp.zeros(tail_ref.shape, jnp.bfloat16)

    @pl.when(step < chunks)
    def _():
        load_operand(count_ref, xr_ref, xi_ref, operand_ref)

        def block_fields(block, sums):
            start = pl.multiple_of(block * rows, rows)
            here = pl.ds(start, rows)
            product = jnp.dot(h_ref[pl.ds(start, rows), :], operand_ref[...], preferred_element_type=jnp.float32)
            real, imag = product[:, :CHUNK], product[:, CHUNK:]
            out_ref[0, here, :] = real
            out_ref[1, here, :] = imag
            power = real * real + imag * imag
            field_ref[here, :] = power.astype(jnp.bfloat16)
            return sums + power_sum(power)

        sums = lax.fori_loop(0, columns // rows, block_fields, jnp.zeros((8, CHUNK), jnp.float32))
        inverse = inverse_rms(sums, columns)
        inverse_ref[...] = jnp.broadcast_to(inverse, inverse_ref.shape)
        azimuth_windows(weights_ref, field_ref, looked_ref, tail_ref, step, [inverse * inverse / (WIN * WIN)])

    @pl.when(step >= chunks)
    def _():
        size = power_ref.shape[0]
        here = pl.ds(pl.multiple_of((step - chunks) * size, size), size)
        for tile, (piece,) in range_windows(weights_ref, looked_ref, tail_ref, here, chunks):
            power_ref[:, tile * LANES:(tile + 1) * LANES] = piece.astype(power_ref.dtype)


def window_scratch(fields, columns, ranges, depth):
    return [
        pltpu.VMEM((2 * depth, 2 * CHUNK), jnp.bfloat16),
        pltpu.VMEM((columns, fields * CHUNK), jnp.bfloat16),
        pltpu.VMEM((fields, columns, ranges), jnp.bfloat16),
        pltpu.VMEM((columns, fields * LANES), jnp.bfloat16),
        pltpu.VMEM((3, CHUNK, CHUNK), jnp.bfloat16),
    ]


def focus(count, h, pings, rows=2048, out_rows=1024):
    columns, depth = h.shape[0], pings.shape[0]
    ranges = pings.shape[1] // 2
    chunks = ranges // CHUNK
    last = chunks - 1
    return pl.pallas_call(
        functools.partial(focus_kernel, chunks=chunks, rows=rows),
        grid=(chunks + columns // out_rows,),
        in_specs=[
            pl.BlockSpec(memory_space=pltpu.SMEM),
            pl.BlockSpec(h.shape, lambda j: (0, 0), pipeline_mode=pl.Buffered(1)),
            pl.BlockSpec((depth, CHUNK), lambda j: (0, jnp.minimum(j, last))),
            pl.BlockSpec((depth, CHUNK), lambda j: (0, chunks + jnp.minimum(j, last))),
        ],
        out_specs=[
            pl.BlockSpec((2, columns, CHUNK), lambda j: (0, 0, jnp.minimum(j, last))),
            pl.BlockSpec((8, CHUNK), lambda j: (0, jnp.minimum(j, last))),
            pl.BlockSpec((out_rows, ranges), lambda j: (jnp.maximum(j - chunks, 0), 0)),
        ],
        out_shape=[
            jax.ShapeDtypeStruct((2, columns, ranges), jnp.float32),
            jax.ShapeDtypeStruct((8, ranges), jnp.float32),
            jax.ShapeDtypeStruct((columns, ranges), jnp.bfloat16),
        ],
        scratch_shapes=window_scratch(1, columns, ranges, depth),
        compiler_params=pltpu.CompilerParams(vmem_limit_bytes=FOCUS_VMEM),
        cost_estimate=pl.CostEstimate(
            flops=8 * columns * depth * ranges, bytes_accessed=32 * 2**20, transcendentals=0
        ),
        name="focus",
    )(count, h, pings, pings)


def compare_kernel(
    count_ref, h_ref, xr_ref, xi_ref, f_ref, inverse_ref, power_ref, coherence_ref, interferogram_ref,
    operand_ref, field_ref, looked_ref, tail_ref, weights_ref, kept_ref, *, chunks, rows
):
    step = pl.program_id(0)
    columns = h_ref.shape[0]
    area = float(WIN * WIN)

    @pl.when(step == 0)
    def _():
        band(weights_ref)
        tail_ref[...] = jnp.zeros(tail_ref.shape, jnp.bfloat16)

    @pl.when(step < chunks)
    def _():
        load_operand(count_ref, xr_ref, xi_ref, operand_ref)

        def block_fields(block, sums):
            start = pl.multiple_of(block * rows, rows)
            product = jnp.dot(h_ref[pl.ds(start, rows), :], operand_ref[...], preferred_element_type=jnp.float32)
            here = pl.ds(start, rows)
            f_real, f_imag = f_ref[0, here, :], f_ref[1, here, :]
            g_real, g_imag = product[:, :CHUNK], product[:, CHUNK:]
            power = g_real * g_real + g_imag * g_imag
            field_ref[here, :CHUNK] = (f_real * g_real + f_imag * g_imag).astype(jnp.bfloat16)
            field_ref[here, CHUNK:2 * CHUNK] = (f_imag * g_real - f_real * g_imag).astype(jnp.bfloat16)
            field_ref[here, 2 * CHUNK:] = power.astype(jnp.bfloat16)
            return sums + power_sum(power)

        sums = lax.fori_loop(0, columns // rows, block_fields, jnp.zeros((8, CHUNK), jnp.float32))
        kept_ref[:, pl.ds(pl.multiple_of(step * CHUNK, CHUNK), CHUNK)] = power_ref[...]
        f_scale = inverse_ref[:1, :]
        g_scale = inverse_rms(sums, columns)
        cross = f_scale * g_scale / area
        scales = [cross, cross, g_scale * g_scale / area]
        azimuth_windows(weights_ref, field_ref, looked_ref, tail_ref, step, scales)

    @pl.when(step >= chunks)
    def _():
        size = coherence_ref.shape[0]
        part = min(size, PART)
        for first in range(0, size, part):
            here = pl.ds(pl.multiple_of((step - chunks) * size + first, part), part)
            rows_here = slice(first, first + part)
            for tile, values in range_windows(weights_ref, looked_ref, tail_ref, here, chunks):
                real, imag, g_power = values
                lanes = slice(tile * LANES, (tile + 1) * LANES)
                interferogram_ref[0, rows_here, lanes] = real.astype(jnp.bfloat16)
                interferogram_ref[1, rows_here, lanes] = imag.astype(jnp.bfloat16)
                power = real * real + imag * imag
                energy = kept_ref[here, lanes].astype(jnp.float32) * g_power + 1e-06 / (area * area)
                coherence_ref[rows_here, lanes] = power * lax.rsqrt(jnp.maximum(power * energy, 1e-37))


def compare(count, h, pings, own, inverse, power, rows=1024, out_rows=512):
    columns, depth = h.shape[0], pings.shape[0]
    ranges = pings.shape[1] // 2
    chunks = ranges // CHUNK
    last = chunks - 1
    return pl.pallas_call(
        functools.partial(compare_kernel, chunks=chunks, rows=rows),
        grid=(chunks + columns // out_rows,),
        in_specs=[
            pl.BlockSpec(memory_space=pltpu.SMEM),
            pl.BlockSpec(h.shape, lambda j: (0, 0), pipeline_mode=pl.Buffered(1)),
            pl.BlockSpec((depth, CHUNK), lambda j: (0, jnp.minimum(j, last))),
            pl.BlockSpec((depth, CHUNK), lambda j: (0, chunks + jnp.minimum(j, last))),
            pl.BlockSpec((2, columns, CHUNK), lambda j: (0, 0, jnp.minimum(j, last))),
            pl.BlockSpec((8, CHUNK), lambda j: (0, jnp.minimum(j, last))),
            pl.BlockSpec((columns, CHUNK), lambda j: (0, jnp.minimum(j, last))),
        ],
        out_specs=[
            pl.BlockSpec((out_rows, ranges), lambda j: (jnp.maximum(j - chunks, 0), 0)),
            pl.BlockSpec((2, out_rows, ranges), lambda j: (0, jnp.maximum(j - chunks, 0), 0)),
        ],
        out_shape=[
            jax.ShapeDtypeStruct((columns, ranges), jnp.float32),
            jax.ShapeDtypeStruct((2, columns, ranges), jnp.bfloat16),
        ],
        scratch_shapes=window_scratch(3, columns, ranges, depth) + [pltpu.VMEM((columns, ranges), jnp.bfloat16)],
        compiler_params=pltpu.CompilerParams(vmem_limit_bytes=COMPARE_VMEM),
        name="compare",
    )(count, h, pings, pings, own, inverse, power)


def body(raw_pings, focus_matrix, start_angle, ping_count):
    columns = focus_matrix.shape[1]
    sectors = raw_pings.shape[0]
    position = lax.axis_index("sector")
    neighbour = (position + 1) % sectors
    received = lax.all_to_all(raw_pings, "sector", split_axis=0, concat_axis=1, tiled=True)[0]
    angle = start_angle[position] - start_angle[neighbour]
    index = (angle * jnp.arange(columns, dtype=jnp.int32)) % columns
    phase = 2.0 * jnp.pi / columns * index.astype(jnp.float32)
    cosine, sine = jnp.cos(phase)[:, None], jnp.sin(phase)[:, None]
    h_real, h_imag = focus_matrix[0].astype(jnp.float32), focus_matrix[1].astype(jnp.float32)
    turned = [h_real * cosine - h_imag * sine, h_real * sine + h_imag * cosine]
    turned = jnp.concatenate([part.astype(jnp.bfloat16) for part in turned], axis=1)
    plain = jnp.concatenate([focus_matrix[0], focus_matrix[1]], axis=1)
    counts = ping_count[jnp.stack([position, neighbour])]
    received, plain, turned, counts = lax.optimization_barrier((received, plain, turned, counts))
    own_pings = received.reshape(received.shape[0], -1)
    other_pings = shifted(own_pings, "sector", -1)
    own, inverse, power = focus(counts[:1], plain, own_pings)
    coherence, interferogram = compare(counts[1:], turned, other_pings, own, inverse, power)
    return (coherence[None], interferogram[None])


def solution(mesh):
    return jax.shard_map(
        body,
        mesh=mesh,
        in_specs=(P("survey", "sector", None, None), P(), P("survey"), P("survey")),
        out_specs=(P(("survey", "sector"), None, None), P(("survey", "sector"), None, None, None)),
        check_vma=False,
    )
```

```python
import functools

import jax
import jax.numpy as jnp
from jax import lax
from jax.experimental import pallas as pl
from jax.experimental.pallas import tpu as pltpu
from jax.sharding import PartitionSpec as P

WIN = 9
LANES = 128
CHUNK = 256
FOCUS_VMEM = 34 * 2**20
FIRST_VMEM = 32 * 2**20
PIECES = 2
COMPARE_VMEM = 44 * 2**20
PART = 512


def shifted(block, axis, distance):
    devices = range(lax.axis_size(axis))
    route = [((i - distance) % len(devices), i) for i in devices]
    return lax.ppermute(block, axis, route)


def load_operand(count_ref, xr_ref, xi_ref, operand_ref):
    depth = xr_ref.shape[0]
    ping = lax.broadcasted_iota(jnp.int32, xr_ref.shape, 0)
    valid = jnp.where(ping < count_ref[0], 1.0, 0.0).astype(jnp.bfloat16)
    real, imag = xr_ref[...] * valid, xi_ref[...] * valid
    operand_ref[:depth, :CHUNK] = real
    operand_ref[:depth, CHUNK:] = imag
    operand_ref[depth:, :CHUNK] = -imag
    operand_ref[depth:, CHUNK:] = real


def band(weights_ref):
    size = weights_ref.shape[1]
    half = WIN // 2
    row = lax.broadcasted_iota(jnp.int32, (size, size), 0)
    column = lax.broadcasted_iota(jnp.int32, (size, size), 1)
    away = jnp.abs(row - column)
    plain = away <= half
    circular = plain | (away >= size - half)
    halves = plain & ((row < LANES) == (column < LANES))
    for index, kept in enumerate((plain, circular, halves)):
        weights_ref[index] = jnp.where(kept, 1.0, 0.0).astype(jnp.bfloat16)


def azimuth_windows(weights_ref, field_ref, looked_ref, tail_ref, base, step, scales):
    halo = 16
    size = weights_ref.shape[1]
    stride = size - 2 * halo
    columns = field_ref.shape[0]
    blocks = (columns - size) // stride + 1
    for block in range(blocks):
        start = block * stride
        low = halo if block else 0
        high = size if block == blocks - 1 else size - halo
        here = pl.ds(start + low, high - low)
        total = jnp.dot(weights_ref[0], field_ref[pl.ds(start, size), :], preferred_element_type=jnp.float32)
        lane = lax.broadcasted_iota(jnp.int32, (high - low, LANES), 1)
        current = lane < LANES - (WIN - 1) * step
        for field, scale in enumerate(scales):
            scaled = total[low:high, field * CHUNK:(field + 1) * CHUNK] * scale
            last = scaled[:, LANES:]
            before = tail_ref[here, field * LANES:(field + 1) * LANES].astype(jnp.float32)
            looked_ref[field, here, pl.ds(base, LANES)] = scaled[:, :LANES].astype(jnp.bfloat16)
            looked_ref[field, here, pl.ds(base + LANES, LANES)] = jnp.where(current, last, before).astype(jnp.bfloat16)
            tail_ref[here, field * LANES:(field + 1) * LANES] = last.astype(jnp.bfloat16)


def range_windows(weights_ref, looked_ref, tail_ref, here, chunks):
    def product(operand, weights):
        return jnp.dot(operand, weights, preferred_element_type=jnp.float32)

    fields = looked_ref.shape[0]
    following = []
    for field in range(0, fields, 2):
        width = LANES * min(2, fields - field)
        edge = product(tail_ref[here, field * LANES:field * LANES + width], weights_ref[2, :width, :width])
        following += [edge[:, start:start + LANES] for start in range(0, width, LANES)]
    lane = lax.broadcasted_iota(jnp.int32, following[0].shape, 1)
    for chunk in reversed(range(chunks)):
        passes = [
            product(looked_ref[field, here, chunk * CHUNK:(chunk + 1) * CHUNK], weights_ref[1 if chunk else 0])
            for field in range(fields)
        ]
        current = lane < LANES - WIN // 2 - (WIN - 1) * chunk
        after = [jnp.where(current, value[:, LANES:], other) for value, other in zip(passes, following)]
        following = [value[:, LANES:] for value in passes]
        yield 2 * chunk + 1, after
        yield 2 * chunk, [value[:, :LANES] for value in passes]


def power_sum(power):
    return jnp.sum(power.reshape(power.shape[0] // 8, 8, power.shape[1]), axis=0)


def inverse_rms(sums, columns):
    return lax.rsqrt(jnp.sum(sums, axis=0, keepdims=True) / columns + 1e-06)


def focus_kernel(
    count_ref, h_ref, *refs, chunks, rows
):
    pieces = refs[:-8]
    out_ref, inverse_ref, power_ref, operand_ref, field_ref, looked_ref, tail_ref, weights_ref = refs[-8:]
    step = pl.program_id(0)
    columns = h_ref.shape[0]

    @pl.when(step == 0)
    def _():
        band(weights_ref)
        tail_ref[...] = jnp.zeros(tail_ref.shape, jnp.bfloat16)

    each = chunks // (len(pieces) // 2)
    for piece in range(len(pieces) // 2):
        @pl.when(step // each == piece)
        def _():
            load_operand(count_ref, pieces[2 * piece], pieces[2 * piece + 1], operand_ref)

    @pl.when(step < chunks)
    def _():
        def block_fields(block, sums):
            start = pl.multiple_of(block * rows, rows)
            here = pl.ds(start, rows)
            product = jnp.dot(h_ref[pl.ds(start, rows), :], operand_ref[...], preferred_element_type=jnp.float32)
            real, imag = product[:, :CHUNK], product[:, CHUNK:]
            out_ref[0, here, :] = real
            out_ref[1, here, :] = imag
            power = real * real + imag * imag
            field_ref[here, :] = power.astype(jnp.bfloat16)
            return sums + power_sum(power)

        sums = lax.fori_loop(0, columns // rows, block_fields, jnp.zeros((8, CHUNK), jnp.float32))
        inverse = inverse_rms(sums, columns)
        inverse_ref[...] = jnp.broadcast_to(inverse, inverse_ref.shape)
        base = pl.multiple_of(step * CHUNK, CHUNK)
        azimuth_windows(weights_ref, field_ref, looked_ref, tail_ref, base, step, [inverse * inverse / (WIN * WIN)])

    @pl.when(step >= chunks)
    def _():
        size = power_ref.shape[0]
        here = pl.ds(pl.multiple_of((step - chunks) * size, size), size)
        for tile, (piece,) in range_windows(weights_ref, looked_ref, tail_ref, here, chunks):
            power_ref[:, tile * LANES:(tile + 1) * LANES] = piece.astype(power_ref.dtype)


def window_scratch(fields, columns, ranges, depth):
    return [
        pltpu.VMEM((2 * depth, 2 * CHUNK), jnp.bfloat16),
        pltpu.VMEM((columns, fields * CHUNK), jnp.bfloat16),
        pltpu.VMEM((fields, columns, ranges), jnp.bfloat16),
        pltpu.VMEM((columns, fields * LANES), jnp.bfloat16),
        pltpu.VMEM((3, CHUNK, CHUNK), jnp.bfloat16),
    ]


def focus(count, h, pings, rows=2048, out_rows=1024):
    columns, depth = h.shape[0], pings[0].shape[0]
    each = pings[0].shape[1] // 2 // CHUNK
    chunks = each * len(pings)
    ranges = chunks * CHUNK
    last = chunks - 1

    def ping_spec(piece, half):
        return pl.BlockSpec((depth, CHUNK), lambda j: (0, half * each + jnp.clip(j - piece * each, 0, each - 1)))

    return pl.pallas_call(
        functools.partial(focus_kernel, chunks=chunks, rows=rows),
        grid=(chunks + columns // out_rows,),
        in_specs=[
            pl.BlockSpec(memory_space=pltpu.SMEM),
            pl.BlockSpec(h.shape, lambda j: (0, 0), pipeline_mode=pl.Buffered(1)),
        ] + [ping_spec(piece, half) for piece in range(len(pings)) for half in range(2)],
        out_specs=[
            pl.BlockSpec((2, columns, CHUNK), lambda j: (0, 0, jnp.minimum(j, last))),
            pl.BlockSpec((8, CHUNK), lambda j: (0, jnp.minimum(j, last))),
            pl.BlockSpec((out_rows, ranges), lambda j: (jnp.maximum(j - chunks, 0), 0)),
        ],
        out_shape=[
            jax.ShapeDtypeStruct((2, columns, ranges), jnp.float32),
            jax.ShapeDtypeStruct((8, ranges), jnp.float32),
            jax.ShapeDtypeStruct((columns, ranges), jnp.bfloat16),
        ],
        scratch_shapes=window_scratch(1, columns, ranges, depth),
        compiler_params=pltpu.CompilerParams(vmem_limit_bytes=FOCUS_VMEM),
        cost_estimate=pl.CostEstimate(
            flops=8 * columns * depth * ranges, bytes_accessed=32 * 2**20, transcendentals=0
        ),
        name="focus",
    )(count, h, *[array for array in pings for _ in range(2)])


def cross_windows(
    count_ref, h_ref, xr_ref, xi_ref, f_ref, inverse_ref, operand_ref, field_ref, looked_ref, tail_ref, weights_ref,
    base, chunk, rows, before=None
):
    columns = h_ref.shape[0]
    area = float(WIN * WIN)
    load_operand(count_ref, xr_ref, xi_ref, operand_ref)

    def block_fields(block, sums):
        start = pl.multiple_of(block * rows, rows)
        product = jnp.dot(h_ref[pl.ds(start, rows), :], operand_ref[...], preferred_element_type=jnp.float32)
        here = pl.ds(start, rows)
        f_real, f_imag = f_ref[0, here, :], f_ref[1, here, :]
        g_real, g_imag = product[:, :CHUNK], product[:, CHUNK:]
        power = g_real * g_real + g_imag * g_imag
        field_ref[here, :CHUNK] = (f_real * g_real + f_imag * g_imag).astype(jnp.bfloat16)
        field_ref[here, CHUNK:2 * CHUNK] = (f_imag * g_real - f_real * g_imag).astype(jnp.bfloat16)
        field_ref[here, 2 * CHUNK:] = power.astype(jnp.bfloat16)
        return sums + power_sum(power)

    sums = lax.fori_loop(0, columns // rows, block_fields, jnp.zeros((8, CHUNK), jnp.float32))
    f_scale = inverse_ref[:1, :]
    g_scale = inverse_rms(sums, columns)
    cross = f_scale * g_scale / area
    if before is not None:
        before()
    scales = [cross, cross, g_scale * g_scale / area]
    azimuth_windows(weights_ref, field_ref, looked_ref, tail_ref, base, chunk, scales)


def first_kernel(
    count_ref, h_ref, xr_ref, xi_ref, f_ref, inverse_ref, looked_ref, tail_ref, operand_ref, field_ref, weights_ref,
    *, rows
):
    step = pl.program_id(0)

    @pl.when(step == 0)
    def _():
        band(weights_ref)
        tail_ref[...] = jnp.zeros(tail_ref.shape, jnp.bfloat16)

    cross_windows(
        count_ref, h_ref, xr_ref, xi_ref, f_ref, inverse_ref,
        operand_ref, field_ref, looked_ref, tail_ref, weights_ref, 0, step, rows
    )


def compare_first(count, h, pings, own, inverse, rows=1024):
    columns, depth = h.shape[0], pings.shape[0]
    chunks = pings.shape[1] // 2 // CHUNK
    fields = 3
    return pl.pallas_call(
        functools.partial(first_kernel, rows=rows),
        grid=(chunks,),
        in_specs=[
            pl.BlockSpec(memory_space=pltpu.SMEM),
            pl.BlockSpec(h.shape, lambda j: (0, 0), pipeline_mode=pl.Buffered(1)),
            pl.BlockSpec((depth, CHUNK), lambda j: (0, j)),
            pl.BlockSpec((depth, CHUNK), lambda j: (0, chunks + j)),
            pl.BlockSpec((2, columns, CHUNK), lambda j: (0, 0, j)),
            pl.BlockSpec((8, CHUNK), lambda j: (0, j)),
        ],
        out_specs=[
            pl.BlockSpec((fields, columns, CHUNK), lambda j: (0, 0, j)),
            pl.BlockSpec((columns, fields * LANES), lambda j: (0, 0)),
        ],
        out_shape=[
            pltpu.HBM((fields, columns, chunks * CHUNK), jnp.bfloat16),
            jax.ShapeDtypeStruct((columns, fields * LANES), jnp.bfloat16),
        ],
        scratch_shapes=[
            pltpu.VMEM((2 * depth, 2 * CHUNK), jnp.bfloat16),
            pltpu.VMEM((columns, fields * CHUNK), jnp.bfloat16),
            pltpu.VMEM((3, CHUNK, CHUNK), jnp.bfloat16),
        ],
        compiler_params=pltpu.CompilerParams(vmem_limit_bytes=FIRST_VMEM),
        cost_estimate=pl.CostEstimate(
            flops=8 * columns * depth * chunks * CHUNK, bytes_accessed=24 * 2**20, transcendentals=0
        ),
        name="compare_first",
    )(count, h, pings, pings, own, inverse)


def compare_kernel(
    count_ref, h_ref, xr_ref, xi_ref, f_ref, inverse_ref, power_ref, begun_ref, edge_ref,
    coherence_ref, interferogram_ref,
    operand_ref, field_ref, looked_ref, tail_ref, weights_ref, kept_ref, sems, *, first, chunks, rows
):
    step = pl.program_id(0)
    area = float(WIN * WIN)
    fresh = chunks - first
    edge_copy = pltpu.make_async_copy(edge_ref, tail_ref, sems.at[0])
    begun_copy = pltpu.make_async_copy(begun_ref, looked_ref.at[:, :, pl.ds(0, first * CHUNK)], sems.at[1])
    power_copy = pltpu.make_async_copy(power_ref, kept_ref, sems.at[2])

    @pl.when(step == 0)
    def _():
        edge_copy.start()
        begun_copy.start()
        power_copy.start()
        band(weights_ref)

    def wait_edge():
        @pl.when(step == 0)
        def _():
            edge_copy.wait()

    @pl.when(step < fresh)
    def _():
        chunk = first + step
        cross_windows(
            count_ref, h_ref, xr_ref, xi_ref, f_ref, inverse_ref,
            operand_ref, field_ref, looked_ref, tail_ref, weights_ref,
            pl.multiple_of(chunk * CHUNK, CHUNK), chunk, rows, wait_edge
        )

    @pl.when(step == fresh)
    def _():
        begun_copy.wait()
        power_copy.wait()

    @pl.when(step >= fresh)
    def _():
        size = coherence_ref.shape[0]
        here = pl.ds(pl.multiple_of((step - fresh) * size, size), size)
        for tile, values in range_windows(weights_ref, looked_ref, tail_ref, here, chunks):
            real, imag, g_power = values
            lanes = slice(tile * LANES, (tile + 1) * LANES)
            interferogram_ref[0, :, lanes] = real.astype(jnp.bfloat16)
            interferogram_ref[1, :, lanes] = imag.astype(jnp.bfloat16)
            power = real * real + imag * imag
            energy = kept_ref[here, lanes].astype(jnp.float32) * g_power + 1e-06 / (area * area)
            coherence_ref[:, lanes] = power * lax.rsqrt(jnp.maximum(power * energy, 1e-37))


def compare(count, h, pings, own, inverse, power, begun, edge, rows=1024, out_rows=512):
    columns, depth = h.shape[0], pings.shape[0]
    ranges = power.shape[1]
    chunks = ranges // CHUNK
    first = begun.shape[2] // CHUNK
    fresh = chunks - first
    last = fresh - 1
    return pl.pallas_call(
        functools.partial(compare_kernel, first=first, chunks=chunks, rows=rows),
        grid=(fresh + columns // out_rows,),
        in_specs=[
            pl.BlockSpec(memory_space=pltpu.SMEM),
            pl.BlockSpec(h.shape, lambda j: (0, 0), pipeline_mode=pl.Buffered(1)),
            pl.BlockSpec((depth, CHUNK), lambda j: (0, jnp.minimum(j, last))),
            pl.BlockSpec((depth, CHUNK), lambda j: (0, fresh + jnp.minimum(j, last))),
            pl.BlockSpec((2, columns, CHUNK), lambda j: (0, 0, first + jnp.minimum(j, last))),
            pl.BlockSpec((8, CHUNK), lambda j: (0, first + jnp.minimum(j, last))),
        ] + [pl.BlockSpec(memory_space=pl.ANY)] * 3,
        out_specs=[
            pl.BlockSpec((out_rows, ranges), lambda j: (jnp.maximum(j - fresh, 0), 0)),
            pl.BlockSpec((2, out_rows, ranges), lambda j: (0, jnp.maximum(j - fresh, 0), 0)),
        ],
        out_shape=[
            jax.ShapeDtypeStruct((columns, ranges), jnp.float32),
            jax.ShapeDtypeStruct((2, columns, ranges), jnp.bfloat16),
        ],
        scratch_shapes=window_scratch(3, columns, ranges, depth) + [
            pltpu.VMEM((columns, ranges), jnp.bfloat16),
            pltpu.SemaphoreType.DMA((3,)),
        ],
        compiler_params=pltpu.CompilerParams(vmem_limit_bytes=COMPARE_VMEM),
        cost_estimate=pl.CostEstimate(
            flops=12 * columns * depth * ranges // 2, bytes_accessed=40 * 2**20, transcendentals=0
        ),
        name="compare",
    )(count, h, pings, pings, own, inverse, power, begun, edge)


def body(raw_pings, focus_matrix, start_angle, ping_count):
    columns = focus_matrix.shape[1]
    sectors = raw_pings.shape[0]
    position = lax.axis_index("sector")
    neighbour = (position + 1) % sectors
    received = lax.all_to_all(raw_pings, "sector", split_axis=0, concat_axis=1, tiled=True)[0]
    angle = start_angle[position] - start_angle[neighbour]
    index = (angle * jnp.arange(columns, dtype=jnp.int32)) % columns
    phase = 2.0 * jnp.pi / columns * index.astype(jnp.float32)
    cosine, sine = jnp.cos(phase)[:, None], jnp.sin(phase)[:, None]
    h_real, h_imag = focus_matrix[0].astype(jnp.float32), focus_matrix[1].astype(jnp.float32)
    turned = [h_real * cosine - h_imag * sine, h_real * sine + h_imag * cosine]
    turned = jnp.concatenate([part.astype(jnp.bfloat16) for part in turned], axis=1)
    plain = jnp.concatenate([focus_matrix[0], focus_matrix[1]], axis=1)
    counts = ping_count[jnp.stack([position, neighbour])]
    received, plain, turned, counts = lax.optimization_barrier((received, plain, turned, counts))
    width = raw_pings.shape[3] // PIECES
    own_pings = [
        received[:, :, piece * width:(piece + 1) * width].reshape(received.shape[0], -1) for piece in range(PIECES)
    ]
    other_pings = [shifted(piece, "sector", -1) for piece in own_pings]
    own, inverse, power = focus(counts[:1], plain, own_pings)
    begun, edge = compare_first(counts[1:], turned, other_pings[0], own, inverse)
    coherence, interferogram = compare(counts[1:], turned, other_pings[1], own, inverse, power, begun, edge)
    return (coherence[None], interferogram[None])


def solution(mesh):
    return jax.shard_map(
        body,
        mesh=mesh,
        in_specs=(P("survey", "sector", None, None), P(), P("survey"), P("survey")),
        out_specs=(P(("survey", "sector"), None, None), P(("survey", "sector"), None, None, None)),
        check_vma=False,
    )
```

```python
import functools

import jax
import jax.numpy as jnp
from jax import lax
from jax.experimental import pallas as pl
from jax.experimental.pallas import tpu as pltpu
from jax.sharding import PartitionSpec as P

WIN = 9
LANES = 128
CHUNK = 256
FOCUS_VMEM = 34 * 2**20
FIRST_VMEM = 32 * 2**20
PIECES = 2
COMPARE_VMEM = 44 * 2**20
PART = 512


def shifted(block, axis, distance):
    devices = range(lax.axis_size(axis))
    route = [((i - distance) % len(devices), i) for i in devices]
    return lax.ppermute(block, axis, route)


def load_operand(count_ref, xr_ref, xi_ref, operand_ref):
    depth = xr_ref.shape[0]
    ping = lax.broadcasted_iota(jnp.int32, xr_ref.shape, 0)
    valid = jnp.where(ping < count_ref[0], 1.0, 0.0).astype(jnp.bfloat16)
    real, imag = xr_ref[...] * valid, xi_ref[...] * valid
    operand_ref[:depth, :CHUNK] = real
    operand_ref[:depth, CHUNK:] = imag
    operand_ref[depth:, :CHUNK] = -imag
    operand_ref[depth:, CHUNK:] = real


def band(weights_ref):
    size = weights_ref.shape[1]
    half = WIN // 2
    row = lax.broadcasted_iota(jnp.int32, (size, size), 0)
    column = lax.broadcasted_iota(jnp.int32, (size, size), 1)
    away = jnp.abs(row - column)
    plain = away <= half
    circular = plain | (away >= size - half)
    halves = plain & ((row < LANES) == (column < LANES))
    for index, kept in enumerate((plain, circular, halves)):
        weights_ref[index] = jnp.where(kept, 1.0, 0.0).astype(jnp.bfloat16)


def azimuth_windows(weights_ref, field_ref, looked_ref, tail_ref, base, step, scales):
    halo = 16
    size = weights_ref.shape[1]
    stride = size - 2 * halo
    columns = field_ref.shape[0]
    blocks = (columns - size) // stride + 1
    for block in range(blocks):
        start = block * stride
        low = halo if block else 0
        high = size if block == blocks - 1 else size - halo
        here = pl.ds(start + low, high - low)
        total = jnp.dot(weights_ref[0], field_ref[pl.ds(start, size), :], preferred_element_type=jnp.float32)
        lane = lax.broadcasted_iota(jnp.int32, (high - low, LANES), 1)
        current = lane < LANES - (WIN - 1) * step
        for field, scale in enumerate(scales):
            scaled = total[low:high, field * CHUNK:(field + 1) * CHUNK] * scale
            last = scaled[:, LANES:]
            before = tail_ref[here, field * LANES:(field + 1) * LANES].astype(jnp.float32)
            looked_ref[field, here, pl.ds(base, LANES)] = scaled[:, :LANES].astype(jnp.bfloat16)
            looked_ref[field, here, pl.ds(base + LANES, LANES)] = jnp.where(current, last, before).astype(jnp.bfloat16)
            tail_ref[here, field * LANES:(field + 1) * LANES] = last.astype(jnp.bfloat16)


def range_windows(weights_ref, looked_ref, tail_ref, here, chunks):
    def product(operand, weights):
        return jnp.dot(operand, weights, preferred_element_type=jnp.float32)

    fields = looked_ref.shape[0]
    following = []
    for field in range(0, fields, 2):
        width = LANES * min(2, fields - field)
        edge = product(tail_ref[here, field * LANES:field * LANES + width], weights_ref[2, :width, :width])
        following += [edge[:, start:start + LANES] for start in range(0, width, LANES)]
    lane = lax.broadcasted_iota(jnp.int32, following[0].shape, 1)
    for chunk in reversed(range(chunks)):
        passes = [
            product(looked_ref[field, here, chunk * CHUNK:(chunk + 1) * CHUNK], weights_ref[1 if chunk else 0])
            for field in range(fields)
        ]
        current = lane < LANES - WIN // 2 - (WIN - 1) * chunk
        after = [jnp.where(current, value[:, LANES:], other) for value, other in zip(passes, following)]
        following = [value[:, LANES:] for value in passes]
        yield 2 * chunk + 1, after
        yield 2 * chunk, [value[:, :LANES] for value in passes]


def power_sum(power):
    return jnp.sum(power.reshape(power.shape[0] // 8, 8, power.shape[1]), axis=0)


def inverse_rms(sums, columns):
    return lax.rsqrt(jnp.sum(sums, axis=0, keepdims=True) / columns + 1e-06)


def focus_kernel(
    count_ref, h_ref, *refs, chunks, rows
):
    pieces = refs[:-8]
    out_ref, inverse_ref, power_ref, operand_ref, field_ref, looked_ref, tail_ref, weights_ref = refs[-8:]
    step = pl.program_id(0)
    columns = h_ref.shape[0]

    @pl.when(step == 0)
    def _():
        band(weights_ref)
        tail_ref[...] = jnp.zeros(tail_ref.shape, jnp.bfloat16)

    each = chunks // (len(pieces) // 2)
    for piece in range(len(pieces) // 2):
        @pl.when(step // each == piece)
        def _():
            load_operand(count_ref, pieces[2 * piece], pieces[2 * piece + 1], operand_ref)

    @pl.when(step < chunks)
    def _():
        def block_fields(block, sums):
            start = pl.multiple_of(block * rows, rows)
            here = pl.ds(start, rows)
            product = jnp.dot(h_ref[pl.ds(start, rows), :], operand_ref[...], preferred_element_type=jnp.float32)
            real, imag = product[:, :CHUNK], product[:, CHUNK:]
            out_ref[0, here, :] = real
            out_ref[1, here, :] = imag
            power = real * real + imag * imag
            field_ref[here, :] = power.astype(jnp.bfloat16)
            return sums + power_sum(power)

        sums = lax.fori_loop(0, columns // rows, block_fields, jnp.zeros((8, CHUNK), jnp.float32))
        inverse = inverse_rms(sums, columns)
        inverse_ref[...] = jnp.broadcast_to(inverse, inverse_ref.shape)
        base = pl.multiple_of(step * CHUNK, CHUNK)
        azimuth_windows(weights_ref, field_ref, looked_ref, tail_ref, base, step, [inverse * inverse / (WIN * WIN)])

    @pl.when(step >= chunks)
    def _():
        size = power_ref.shape[0]
        here = pl.ds(pl.multiple_of((step - chunks) * size, size), size)
        for tile, (piece,) in range_windows(weights_ref, looked_ref, tail_ref, here, chunks):
            power_ref[:, tile * LANES:(tile + 1) * LANES] = piece.astype(power_ref.dtype)


def window_scratch(fields, columns, ranges, depth):
    return [
        pltpu.VMEM((2 * depth, 2 * CHUNK), jnp.bfloat16),
        pltpu.VMEM((columns, fields * CHUNK), jnp.bfloat16),
        pltpu.VMEM((fields, columns, ranges), jnp.bfloat16),
        pltpu.VMEM((columns, fields * LANES), jnp.bfloat16),
        pltpu.VMEM((3, CHUNK, CHUNK), jnp.bfloat16),
    ]


def focus(count, h, pings, rows=2048, out_rows=1024):
    columns, depth = h.shape[0], pings[0].shape[0]
    each = pings[0].shape[1] // 2 // CHUNK
    chunks = each * len(pings)
    ranges = chunks * CHUNK
    last = chunks - 1

    def ping_spec(piece, half):
        return pl.BlockSpec((depth, CHUNK), lambda j: (0, half * each + jnp.clip(j - piece * each, 0, each - 1)))

    return pl.pallas_call(
        functools.partial(focus_kernel, chunks=chunks, rows=rows),
        grid=(chunks + columns // out_rows,),
        in_specs=[
            pl.BlockSpec(memory_space=pltpu.SMEM),
            pl.BlockSpec(h.shape, lambda j: (0, 0), pipeline_mode=pl.Buffered(1)),
        ] + [ping_spec(piece, half) for piece in range(len(pings)) for half in range(2)],
        out_specs=[
            pl.BlockSpec((2, columns, CHUNK), lambda j: (0, 0, jnp.minimum(j, last))),
            pl.BlockSpec((8, CHUNK), lambda j: (0, jnp.minimum(j, last))),
            pl.BlockSpec((out_rows, ranges), lambda j: (jnp.maximum(j - chunks, 0), 0)),
        ],
        out_shape=[
            jax.ShapeDtypeStruct((2, columns, ranges), jnp.float32),
            jax.ShapeDtypeStruct((8, ranges), jnp.float32),
            jax.ShapeDtypeStruct((columns, ranges), jnp.bfloat16),
        ],
        scratch_shapes=window_scratch(1, columns, ranges, depth),
        compiler_params=pltpu.CompilerParams(vmem_limit_bytes=FOCUS_VMEM),
        cost_estimate=pl.CostEstimate(
            flops=8 * columns * depth * ranges, bytes_accessed=32 * 2**20, transcendentals=0
        ),
        name="focus",
    )(count, h, *[array for array in pings for _ in range(2)])


def cross_windows(
    count_ref, h_ref, xr_ref, xi_ref, f_ref, inverse_ref, operand_ref, field_ref, looked_ref, tail_ref, weights_ref,
    base, chunk, rows, before=None
):
    columns = h_ref.shape[0]
    area = float(WIN * WIN)
    load_operand(count_ref, xr_ref, xi_ref, operand_ref)

    def block_fields(block, sums):
        start = pl.multiple_of(block * rows, rows)
        product = jnp.dot(h_ref[pl.ds(start, rows), :], operand_ref[...], preferred_element_type=jnp.float32)
        here = pl.ds(start, rows)
        f_real, f_imag = f_ref[0, here, :], f_ref[1, here, :]
        g_real, g_imag = product[:, :CHUNK], product[:, CHUNK:]
        power = g_real * g_real + g_imag * g_imag
        field_ref[here, :CHUNK] = (f_real * g_real + f_imag * g_imag).astype(jnp.bfloat16)
        field_ref[here, CHUNK:2 * CHUNK] = (f_imag * g_real - f_real * g_imag).astype(jnp.bfloat16)
        field_ref[here, 2 * CHUNK:] = power.astype(jnp.bfloat16)
        return sums + power_sum(power)

    sums = lax.fori_loop(0, columns // rows, block_fields, jnp.zeros((8, CHUNK), jnp.float32))
    f_scale = inverse_ref[:1, :]
    g_scale = inverse_rms(sums, columns)
    cross = f_scale * g_scale / area
    if before is not None:
        before()
    scales = [cross, cross, g_scale * g_scale / area]
    azimuth_windows(weights_ref, field_ref, looked_ref, tail_ref, base, chunk, scales)


def first_kernel(
    count_ref, h_ref, xr_ref, xi_ref, f_ref, inverse_ref, looked_ref, tail_ref, operand_ref, field_ref, weights_ref,
    *, rows
):
    step = pl.program_id(0)

    @pl.when(step == 0)
    def _():
        band(weights_ref)
        tail_ref[...] = jnp.zeros(tail_ref.shape, jnp.bfloat16)

    cross_windows(
        count_ref, h_ref, xr_ref, xi_ref, f_ref, inverse_ref,
        operand_ref, field_ref, looked_ref, tail_ref, weights_ref, 0, step, rows
    )


def compare_first(count, h, pings, own, inverse, rows=1024):
    columns, depth = h.shape[0], pings.shape[0]
    chunks = pings.shape[1] // 2 // CHUNK
    fields = 3
    return pl.pallas_call(
        functools.partial(first_kernel, rows=rows),
        grid=(chunks,),
        in_specs=[
            pl.BlockSpec(memory_space=pltpu.SMEM),
            pl.BlockSpec(h.shape, lambda j: (0, 0), pipeline_mode=pl.Buffered(1)),
            pl.BlockSpec((depth, CHUNK), lambda j: (0, j)),
            pl.BlockSpec((depth, CHUNK), lambda j: (0, chunks + j)),
            pl.BlockSpec((2, columns, CHUNK), lambda j: (0, 0, j)),
            pl.BlockSpec((8, CHUNK), lambda j: (0, j)),
        ],
        out_specs=[
            pl.BlockSpec((fields, columns, CHUNK), lambda j: (0, 0, j)),
            pl.BlockSpec((columns, fields * LANES), lambda j: (0, 0)),
        ],
        out_shape=[
            pltpu.HBM((fields, columns, chunks * CHUNK), jnp.bfloat16),
            jax.ShapeDtypeStruct((columns, fields * LANES), jnp.bfloat16),
        ],
        scratch_shapes=[
            pltpu.VMEM((2 * depth, 2 * CHUNK), jnp.bfloat16),
            pltpu.VMEM((columns, fields * CHUNK), jnp.bfloat16),
            pltpu.VMEM((3, CHUNK, CHUNK), jnp.bfloat16),
        ],
        compiler_params=pltpu.CompilerParams(vmem_limit_bytes=FIRST_VMEM),
        cost_estimate=pl.CostEstimate(
            flops=8 * columns * depth * chunks * CHUNK, bytes_accessed=24 * 2**20, transcendentals=0
        ),
        name="compare_first",
    )(count, h, pings, pings, own, inverse)


def compare_kernel(
    count_ref, h_ref, xr_ref, xi_ref, f_ref, inverse_ref, power_ref, begun_ref, edge_ref,
    coherence_ref, interferogram_ref,
    operand_ref, field_ref, looked_ref, tail_ref, weights_ref, kept_ref, sems, *, first, chunks, rows
):
    step = pl.program_id(0)
    area = float(WIN * WIN)
    fresh = chunks - first
    edge_copy = pltpu.make_async_copy(edge_ref, tail_ref, sems.at[0])
    begun_copy = pltpu.make_async_copy(begun_ref, looked_ref.at[:, :, pl.ds(0, first * CHUNK)], sems.at[1])
    power_copy = pltpu.make_async_copy(power_ref, kept_ref, sems.at[2])

    @pl.when(step == 0)
    def _():
        edge_copy.start()
        begun_copy.start()
        power_copy.start()
        band(weights_ref)

    def wait_edge():
        @pl.when(step == 0)
        def _():
            edge_copy.wait()

    @pl.when(step < fresh)
    def _():
        chunk = first + step
        cross_windows(
            count_ref, h_ref, xr_ref, xi_ref, f_ref, inverse_ref,
            operand_ref, field_ref, looked_ref, tail_ref, weights_ref,
            pl.multiple_of(chunk * CHUNK, CHUNK), chunk, rows, wait_edge
        )

    @pl.when(step == fresh)
    def _():
        begun_copy.wait()
        power_copy.wait()

    @pl.when(step >= fresh)
    def _():
        size = coherence_ref.shape[0]
        here = pl.ds(pl.multiple_of((step - fresh) * size, size), size)
        for tile, values in range_windows(weights_ref, looked_ref, tail_ref, here, chunks):
            real, imag, g_power = values
            lanes = slice(tile * LANES, (tile + 1) * LANES)
            interferogram_ref[0, :, lanes] = real.astype(jnp.bfloat16)
            interferogram_ref[1, :, lanes] = imag.astype(jnp.bfloat16)
            power = real * real + imag * imag
            energy = kept_ref[here, lanes].astype(jnp.float32) * g_power + 1e-06 / (area * area)
            coherence_ref[:, lanes] = power * lax.rsqrt(jnp.maximum(power * energy, 1e-37))


def compare(count, h, pings, own, inverse, power, begun, edge, rows=1024, out_rows=512):
    columns, depth = h.shape[0], pings.shape[0]
    ranges = power.shape[1]
    chunks = ranges // CHUNK
    first = begun.shape[2] // CHUNK
    fresh = chunks - first
    last = fresh - 1
    return pl.pallas_call(
        functools.partial(compare_kernel, first=first, chunks=chunks, rows=rows),
        grid=(fresh + columns // out_rows,),
        in_specs=[
            pl.BlockSpec(memory_space=pltpu.SMEM),
            pl.BlockSpec(h.shape, lambda j: (0, 0), pipeline_mode=pl.Buffered(1)),
            pl.BlockSpec((depth, CHUNK), lambda j: (0, jnp.minimum(j, last))),
            pl.BlockSpec((depth, CHUNK), lambda j: (0, fresh + jnp.minimum(j, last))),
            pl.BlockSpec((2, columns, CHUNK), lambda j: (0, 0, first + jnp.minimum(j, last))),
            pl.BlockSpec((8, CHUNK), lambda j: (0, first + jnp.minimum(j, last))),
        ] + [pl.BlockSpec(memory_space=pl.ANY)] * 3,
        out_specs=[
            pl.BlockSpec((out_rows, ranges), lambda j: (jnp.maximum(j - fresh, 0), 0)),
            pl.BlockSpec((2, out_rows, ranges), lambda j: (0, jnp.maximum(j - fresh, 0), 0)),
        ],
        out_shape=[
            jax.ShapeDtypeStruct((columns, ranges), jnp.float32),
            jax.ShapeDtypeStruct((2, columns, ranges), jnp.bfloat16),
        ],
        scratch_shapes=window_scratch(3, columns, ranges, depth) + [
            pltpu.VMEM((columns, ranges), jnp.bfloat16),
            pltpu.SemaphoreType.DMA((3,)),
        ],
        compiler_params=pltpu.CompilerParams(vmem_limit_bytes=COMPARE_VMEM),
        cost_estimate=pl.CostEstimate(
            flops=12 * columns * depth * ranges // 2, bytes_accessed=40 * 2**20, transcendentals=0
        ),
        name="compare",
    )(count, h, pings, pings, own, inverse, power, begun, edge)


def body(raw_pings, focus_matrix, start_angle, ping_count):
    columns = focus_matrix.shape[1]
    sectors = raw_pings.shape[0]
    position = lax.axis_index("sector")
    neighbour = (position + 1) % sectors
    received = lax.all_to_all(raw_pings, "sector", split_axis=0, concat_axis=1, tiled=True)[0]
    angle = start_angle[position] - start_angle[neighbour]
    index = (angle * jnp.arange(columns, dtype=jnp.int32)) % columns
    phase = 2.0 * jnp.pi / columns * index.astype(jnp.float32)
    cosine, sine = jnp.cos(phase)[:, None], jnp.sin(phase)[:, None]
    h_real, h_imag = focus_matrix[0].astype(jnp.float32), focus_matrix[1].astype(jnp.float32)
    turned = [h_real * cosine - h_imag * sine, h_real * sine + h_imag * cosine]
    turned = jnp.concatenate([part.astype(jnp.bfloat16) for part in turned], axis=1)
    plain = jnp.concatenate([focus_matrix[0], focus_matrix[1]], axis=1)
    own_count = lax.dynamic_slice_in_dim(ping_count, position, 1)
    other_count = lax.dynamic_slice_in_dim(ping_count, neighbour, 1)
    received, plain, turned, own_count, other_count = lax.optimization_barrier(
        (received, plain, turned, own_count, other_count)
    )
    width = raw_pings.shape[3] // PIECES
    own_pings = [
        received[:, :, piece * width:(piece + 1) * width].reshape(received.shape[0], -1) for piece in range(PIECES)
    ]
    other_pings = [shifted(piece, "sector", -1) for piece in own_pings]
    own, inverse, power = focus(own_count, plain, own_pings)
    begun, edge = compare_first(other_count, turned, other_pings[0], own, inverse)
    coherence, interferogram = compare(other_count, turned, other_pings[1], own, inverse, power, begun, edge)
    return (coherence[None], interferogram[None])


def solution(mesh):
    return jax.shard_map(
        body,
        mesh=mesh,
        in_specs=(P("survey", "sector", None, None), P(), P("survey"), P("survey")),
        out_specs=(P(("survey", "sector"), None, None), P(("survey", "sector"), None, None, None)),
        check_vma=False,
    )
```

```python
import functools

import jax
import jax.numpy as jnp
from jax import lax
from jax.experimental import pallas as pl
from jax.experimental.pallas import tpu as pltpu
from jax.sharding import PartitionSpec as P

WIN = 9
LANES = 128
CHUNK = 256
FOCUS_VMEM = 34 * 2**20
FIRST_VMEM = 32 * 2**20
PIECES = 2
COMPARE_VMEM = 44 * 2**20
PART = 512


def shifted(block, axis, distance):
    devices = range(lax.axis_size(axis))
    route = [((i - distance) % len(devices), i) for i in devices]
    return lax.ppermute(block, axis, route)


def load_operand(count_ref, xr_ref, xi_ref, operand_ref):
    depth = xr_ref.shape[0]
    ping = lax.broadcasted_iota(jnp.int32, xr_ref.shape, 0)
    valid = jnp.where(ping < count_ref[0], 1.0, 0.0).astype(jnp.bfloat16)
    real, imag = xr_ref[...] * valid, xi_ref[...] * valid
    operand_ref[:depth, :CHUNK] = real
    operand_ref[:depth, CHUNK:] = imag
    operand_ref[depth:, :CHUNK] = -imag
    operand_ref[depth:, CHUNK:] = real


def band(weights_ref):
    size = weights_ref.shape[1]
    half = WIN // 2
    row = lax.broadcasted_iota(jnp.int32, (size, size), 0)
    column = lax.broadcasted_iota(jnp.int32, (size, size), 1)
    away = jnp.abs(row - column)
    plain = away <= half
    circular = plain | (away >= size - half)
    halves = plain & ((row < LANES) == (column < LANES))
    for index, kept in enumerate((plain, circular, halves)):
        weights_ref[index] = jnp.where(kept, 1.0, 0.0).astype(jnp.bfloat16)


def azimuth_windows(weights_ref, field_ref, looked_ref, tail_ref, base, step, scales):
    halo = 16
    size = weights_ref.shape[1]
    stride = size - 2 * halo
    columns = field_ref.shape[0]
    blocks = (columns - size) // stride + 1
    for block in range(blocks):
        start = block * stride
        low = halo if block else 0
        high = size if block == blocks - 1 else size - halo
        here = pl.ds(start + low, high - low)
        total = jnp.dot(weights_ref[0], field_ref[pl.ds(start, size), :], preferred_element_type=jnp.float32)
        lane = lax.broadcasted_iota(jnp.int32, (high - low, LANES), 1)
        current = lane < LANES - (WIN - 1) * step
        for field, scale in enumerate(scales):
            scaled = total[low:high, field * CHUNK:(field + 1) * CHUNK] * scale
            last = scaled[:, LANES:]
            before = tail_ref[here, field * LANES:(field + 1) * LANES].astype(jnp.float32)
            looked_ref[field, here, pl.ds(base, LANES)] = scaled[:, :LANES].astype(jnp.bfloat16)
            looked_ref[field, here, pl.ds(base + LANES, LANES)] = jnp.where(current, last, before).astype(jnp.bfloat16)
            tail_ref[here, field * LANES:(field + 1) * LANES] = last.astype(jnp.bfloat16)


def range_windows(weights_ref, looked_ref, tail_ref, here, chunks):
    def product(operand, weights):
        return jnp.dot(operand, weights, preferred_element_type=jnp.float32)

    fields = looked_ref.shape[0]
    following = []
    for field in range(0, fields, 2):
        width = LANES * min(2, fields - field)
        edge = product(tail_ref[here, field * LANES:field * LANES + width], weights_ref[2, :width, :width])
        following += [edge[:, start:start + LANES] for start in range(0, width, LANES)]
    lane = lax.broadcasted_iota(jnp.int32, following[0].shape, 1)
    for chunk in reversed(range(chunks)):
        passes = [
            product(looked_ref[field, here, chunk * CHUNK:(chunk + 1) * CHUNK], weights_ref[1 if chunk else 0])
            for field in range(fields)
        ]
        current = lane < LANES - WIN // 2 - (WIN - 1) * chunk
        after = [jnp.where(current, value[:, LANES:], other) for value, other in zip(passes, following)]
        following = [value[:, LANES:] for value in passes]
        yield 2 * chunk + 1, after
        yield 2 * chunk, [value[:, :LANES] for value in passes]


def power_sum(power):
    return jnp.sum(power.reshape(power.shape[0] // 8, 8, power.shape[1]), axis=0)


def inverse_rms(sums, columns):
    return lax.rsqrt(jnp.sum(sums, axis=0, keepdims=True) / columns + 1e-06)


def focus_kernel(
    count_ref, h_ref, *refs, chunks, rows
):
    pieces = refs[:-8]
    out_ref, inverse_ref, power_ref, operand_ref, field_ref, looked_ref, tail_ref, weights_ref = refs[-8:]
    step = pl.program_id(0)
    columns = h_ref.shape[0]

    @pl.when(step == 0)
    def _():
        band(weights_ref)
        tail_ref[...] = jnp.zeros(tail_ref.shape, jnp.bfloat16)

    each = chunks // (len(pieces) // 2)
    for piece in range(len(pieces) // 2):
        @pl.when(step // each == piece)
        def _():
            load_operand(count_ref, pieces[2 * piece], pieces[2 * piece + 1], operand_ref)

    @pl.when(step < chunks)
    def _():
        def block_fields(block, sums):
            start = pl.multiple_of(block * rows, rows)
            here = pl.ds(start, rows)
            product = jnp.dot(h_ref[pl.ds(start, rows), :], operand_ref[...], preferred_element_type=jnp.float32)
            real, imag = product[:, :CHUNK], product[:, CHUNK:]
            out_ref[0, here, :] = real
            out_ref[1, here, :] = imag
            power = real * real + imag * imag
            field_ref[here, :] = power.astype(jnp.bfloat16)
            return sums + power_sum(power)

        sums = lax.fori_loop(0, columns // rows, block_fields, jnp.zeros((8, CHUNK), jnp.float32))
        inverse = inverse_rms(sums, columns)
        inverse_ref[...] = jnp.broadcast_to(inverse, inverse_ref.shape)
        base = pl.multiple_of(step * CHUNK, CHUNK)
        azimuth_windows(weights_ref, field_ref, looked_ref, tail_ref, base, step, [inverse * inverse / (WIN * WIN)])

    @pl.when(step >= chunks)
    def _():
        size = power_ref.shape[0]
        here = pl.ds(pl.multiple_of((step - chunks) * size, size), size)
        for tile, (piece,) in range_windows(weights_ref, looked_ref, tail_ref, here, chunks):
            power_ref[:, tile * LANES:(tile + 1) * LANES] = piece.astype(power_ref.dtype)


def window_scratch(fields, columns, ranges, depth):
    return [
        pltpu.VMEM((2 * depth, 2 * CHUNK), jnp.bfloat16),
        pltpu.VMEM((columns, fields * CHUNK), jnp.bfloat16),
        pltpu.VMEM((fields, columns, ranges), jnp.bfloat16),
        pltpu.VMEM((columns, fields * LANES), jnp.bfloat16),
        pltpu.VMEM((3, CHUNK, CHUNK), jnp.bfloat16),
    ]


def focus(count, h, pings, rows=2048, out_rows=1024):
    columns, depth = h.shape[0], pings[0].shape[0]
    each = pings[0].shape[1] // 2 // CHUNK
    chunks = each * len(pings)
    ranges = chunks * CHUNK
    last = chunks - 1

    def ping_spec(piece, half):
        return pl.BlockSpec((depth, CHUNK), lambda j: (0, half * each + jnp.clip(j - piece * each, 0, each - 1)))

    return pl.pallas_call(
        functools.partial(focus_kernel, chunks=chunks, rows=rows),
        grid=(chunks + columns // out_rows,),
        in_specs=[
            pl.BlockSpec(memory_space=pltpu.SMEM),
            pl.BlockSpec(h.shape, lambda j: (0, 0), pipeline_mode=pl.Buffered(1)),
        ] + [ping_spec(piece, half) for piece in range(len(pings)) for half in range(2)],
        out_specs=[
            pl.BlockSpec((2, columns, CHUNK), lambda j: (0, 0, jnp.minimum(j, last))),
            pl.BlockSpec((8, CHUNK), lambda j: (0, jnp.minimum(j, last))),
            pl.BlockSpec((out_rows, ranges), lambda j: (jnp.maximum(j - chunks, 0), 0)),
        ],
        out_shape=[
            jax.ShapeDtypeStruct((2, columns, ranges), jnp.float32),
            jax.ShapeDtypeStruct((8, ranges), jnp.float32),
            jax.ShapeDtypeStruct((columns, ranges), jnp.bfloat16),
        ],
        scratch_shapes=window_scratch(1, columns, ranges, depth),
        compiler_params=pltpu.CompilerParams(vmem_limit_bytes=FOCUS_VMEM),
        cost_estimate=pl.CostEstimate(
            flops=8 * columns * depth * ranges, bytes_accessed=32 * 2**20, transcendentals=0
        ),
        name="focus",
    )(count, h, *[array for array in pings for _ in range(2)])


def cross_windows(
    count_ref, h_ref, xr_ref, xi_ref, f_ref, inverse_ref, operand_ref, field_ref, looked_ref, tail_ref, weights_ref,
    base, chunk, rows, before=None
):
    columns = h_ref.shape[0]
    area = float(WIN * WIN)
    load_operand(count_ref, xr_ref, xi_ref, operand_ref)

    def block_fields(block, sums):
        start = pl.multiple_of(block * rows, rows)
        product = jnp.dot(h_ref[pl.ds(start, rows), :], operand_ref[...], preferred_element_type=jnp.float32)
        here = pl.ds(start, rows)
        f_real, f_imag = f_ref[0, here, :], f_ref[1, here, :]
        g_real, g_imag = product[:, :CHUNK], product[:, CHUNK:]
        power = g_real * g_real + g_imag * g_imag
        field_ref[here, :CHUNK] = (f_real * g_real + f_imag * g_imag).astype(jnp.bfloat16)
        field_ref[here, CHUNK:2 * CHUNK] = (f_imag * g_real - f_real * g_imag).astype(jnp.bfloat16)
        field_ref[here, 2 * CHUNK:] = power.astype(jnp.bfloat16)
        return sums + power_sum(power)

    sums = lax.fori_loop(0, columns // rows, block_fields, jnp.zeros((8, CHUNK), jnp.float32))
    f_scale = inverse_ref[:1, :]
    g_scale = inverse_rms(sums, columns)
    cross = f_scale * g_scale / area
    if before is not None:
        before()
    scales = [cross, cross, g_scale * g_scale / area]
    azimuth_windows(weights_ref, field_ref, looked_ref, tail_ref, base, chunk, scales)


def first_kernel(
    count_ref, h_ref, xr_ref, xi_ref, f_ref, inverse_ref, looked_ref, tail_ref, operand_ref, field_ref, weights_ref,
    *, rows
):
    step = pl.program_id(0)

    @pl.when(step == 0)
    def _():
        band(weights_ref)
        tail_ref[...] = jnp.zeros(tail_ref.shape, jnp.bfloat16)

    cross_windows(
        count_ref, h_ref, xr_ref, xi_ref, f_ref, inverse_ref,
        operand_ref, field_ref, looked_ref, tail_ref, weights_ref, 0, step, rows
    )


def compare_first(count, h, pings, own, inverse, rows=1024):
    columns, depth = h.shape[0], pings.shape[0]
    chunks = pings.shape[1] // 2 // CHUNK
    fields = 3
    return pl.pallas_call(
        functools.partial(first_kernel, rows=rows),
        grid=(chunks,),
        in_specs=[
            pl.BlockSpec(memory_space=pltpu.SMEM),
            pl.BlockSpec(h.shape, lambda j: (0, 0), pipeline_mode=pl.Buffered(1)),
            pl.BlockSpec((depth, CHUNK), lambda j: (0, j)),
            pl.BlockSpec((depth, CHUNK), lambda j: (0, chunks + j)),
            pl.BlockSpec((2, columns, CHUNK), lambda j: (0, 0, j)),
            pl.BlockSpec((8, CHUNK), lambda j: (0, j)),
        ],
        out_specs=[
            pl.BlockSpec((fields, columns, CHUNK), lambda j: (0, 0, j)),
            pl.BlockSpec((columns, fields * LANES), lambda j: (0, 0)),
        ],
        out_shape=[
            pltpu.HBM((fields, columns, chunks * CHUNK), jnp.bfloat16),
            jax.ShapeDtypeStruct((columns, fields * LANES), jnp.bfloat16),
        ],
        scratch_shapes=[
            pltpu.VMEM((2 * depth, 2 * CHUNK), jnp.bfloat16),
            pltpu.VMEM((columns, fields * CHUNK), jnp.bfloat16),
            pltpu.VMEM((3, CHUNK, CHUNK), jnp.bfloat16),
        ],
        compiler_params=pltpu.CompilerParams(vmem_limit_bytes=FIRST_VMEM),
        cost_estimate=pl.CostEstimate(
            flops=8 * columns * depth * chunks * CHUNK, bytes_accessed=24 * 2**20, transcendentals=0
        ),
        name="compare_first",
    )(count, h, pings, pings, own, inverse)


def compare_kernel(
    count_ref, h_ref, xr_ref, xi_ref, f_ref, inverse_ref, power_ref, begun_ref, edge_ref,
    coherence_ref, interferogram_ref,
    operand_ref, field_ref, looked_ref, tail_ref, weights_ref, kept_ref, sems, *, first, chunks, rows
):
    step = pl.program_id(0)
    area = float(WIN * WIN)
    fresh = chunks - first
    edge_copy = pltpu.make_async_copy(edge_ref, tail_ref, sems.at[0])
    begun_copy = pltpu.make_async_copy(begun_ref, looked_ref.at[:, :, pl.ds(0, first * CHUNK)], sems.at[1])
    power_copy = pltpu.make_async_copy(power_ref, kept_ref, sems.at[2])

    @pl.when(step == 0)
    def _():
        edge_copy.start()
        begun_copy.start()
        power_copy.start()
        band(weights_ref)

    def wait_edge():
        @pl.when(step == 0)
        def _():
            edge_copy.wait()

    @pl.when(step < fresh)
    def _():
        chunk = first + step
        cross_windows(
            count_ref, h_ref, xr_ref, xi_ref, f_ref, inverse_ref,
            operand_ref, field_ref, looked_ref, tail_ref, weights_ref,
            pl.multiple_of(chunk * CHUNK, CHUNK), chunk, rows, wait_edge
        )

    @pl.when(step == fresh)
    def _():
        begun_copy.wait()
        power_copy.wait()

    @pl.when(step >= fresh)
    def _():
        size = coherence_ref.shape[0]
        here = pl.ds(pl.multiple_of((step - fresh) * size, size), size)
        for tile, values in range_windows(weights_ref, looked_ref, tail_ref, here, chunks):
            real, imag, g_power = values
            lanes = slice(tile * LANES, (tile + 1) * LANES)
            interferogram_ref[0, :, lanes] = real.astype(jnp.bfloat16)
            interferogram_ref[1, :, lanes] = imag.astype(jnp.bfloat16)
            power = real * real + imag * imag
            energy = kept_ref[here, lanes].astype(jnp.float32) * g_power + 1e-06 / (area * area)
            coherence_ref[:, lanes] = power * lax.rsqrt(jnp.maximum(power * energy, 1e-37))


def compare(count, h, pings, own, inverse, power, begun, edge, rows=1024, out_rows=512):
    columns, depth = h.shape[0], pings.shape[0]
    ranges = power.shape[1]
    chunks = ranges // CHUNK
    first = begun.shape[2] // CHUNK
    fresh = chunks - first
    last = fresh - 1
    return pl.pallas_call(
        functools.partial(compare_kernel, first=first, chunks=chunks, rows=rows),
        grid=(fresh + columns // out_rows,),
        in_specs=[
            pl.BlockSpec(memory_space=pltpu.SMEM),
            pl.BlockSpec(h.shape, lambda j: (0, 0), pipeline_mode=pl.Buffered(1)),
            pl.BlockSpec((depth, CHUNK), lambda j: (0, jnp.minimum(j, last))),
            pl.BlockSpec((depth, CHUNK), lambda j: (0, fresh + jnp.minimum(j, last))),
            pl.BlockSpec((2, columns, CHUNK), lambda j: (0, 0, first + jnp.minimum(j, last))),
            pl.BlockSpec((8, CHUNK), lambda j: (0, first + jnp.minimum(j, last))),
        ] + [pl.BlockSpec(memory_space=pl.ANY)] * 3,
        out_specs=[
            pl.BlockSpec((out_rows, ranges), lambda j: (jnp.maximum(j - fresh, 0), 0)),
            pl.BlockSpec((2, out_rows, ranges), lambda j: (0, jnp.maximum(j - fresh, 0), 0)),
        ],
        out_shape=[
            jax.ShapeDtypeStruct((columns, ranges), jnp.float32),
            jax.ShapeDtypeStruct((2, columns, ranges), jnp.bfloat16),
        ],
        scratch_shapes=window_scratch(3, columns, ranges, depth) + [
            pltpu.VMEM((columns, ranges), jnp.bfloat16),
            pltpu.SemaphoreType.DMA((3,)),
        ],
        compiler_params=pltpu.CompilerParams(vmem_limit_bytes=COMPARE_VMEM),
        cost_estimate=pl.CostEstimate(
            flops=12 * columns * depth * ranges // 2, bytes_accessed=40 * 2**20, transcendentals=0
        ),
        name="compare",
    )(count, h, pings, pings, own, inverse, power, begun, edge)


def body(raw_pings, focus_matrix, start_angle, ping_count):
    columns = focus_matrix.shape[1]
    sectors = raw_pings.shape[0]
    position = lax.axis_index("sector")
    neighbour = (position + 1) % sectors
    received = lax.all_to_all(raw_pings, "sector", split_axis=0, concat_axis=1, tiled=True)[0]
    angle = start_angle[position] - start_angle[neighbour]
    index = (angle * jnp.arange(columns, dtype=jnp.int32)) % columns
    phase = 2.0 * jnp.pi / columns * index.astype(jnp.float32)
    cosine, sine = jnp.cos(phase)[:, None], jnp.sin(phase)[:, None]
    h_real, h_imag = focus_matrix[0].astype(jnp.float32), focus_matrix[1].astype(jnp.float32)
    turned = [h_real * cosine - h_imag * sine, h_real * sine + h_imag * cosine]
    turned = jnp.concatenate([part.astype(jnp.bfloat16) for part in turned], axis=1)
    plain = jnp.concatenate([focus_matrix[0], focus_matrix[1]], axis=1)
    own_count = lax.dynamic_slice_in_dim(ping_count, position, 1)
    other_count = lax.dynamic_slice_in_dim(ping_count, neighbour, 1)
    received, plain, turned, own_count, other_count = lax.optimization_barrier(
        (received, plain, turned, own_count, other_count)
    )
    width = raw_pings.shape[3] // PIECES
    own_pings = []
    for piece in range(PIECES):
        part = received[:, :, piece * width:(piece + 1) * width].reshape(received.shape[0], -1)
        part, received = lax.optimization_barrier((part, received))
        own_pings.append(part)
    other_pings = [shifted(piece, "sector", -1) for piece in own_pings]
    own, inverse, power = focus(own_count, plain, own_pings)
    begun, edge = compare_first(other_count, turned, other_pings[0], own, inverse)
    coherence, interferogram = compare(other_count, turned, other_pings[1], own, inverse, power, begun, edge)
    return (coherence[None], interferogram[None])


def solution(mesh):
    return jax.shard_map(
        body,
        mesh=mesh,
        in_specs=(P("survey", "sector", None, None), P(), P("survey"), P("survey")),
        out_specs=(P(("survey", "sector"), None, None), P(("survey", "sector"), None, None, None)),
        check_vma=False,
    )
```
